32 devices in a mesh: basin: 2 (over x), recv: 8 (over z, y), src: 2 (over core).
Axes of the slice: x: 2, y: 2, z: 4, core: 2. Of those that a mesh axis runs over, the one named last changes fastest.
Arguments:
- positions: float32 [3, 4096], P(None, ('basin', 'recv', 'src')), parts along dimension 1, may hold values from -1.1 to 1.1, as said below
- normals: float32 [3, 4096], P(None, ('basin', 'recv', 'src')), parts along dimension 1, may hold values from -1 to 1, as said below
- area: float32 [4096], P(('basin', 'recv', 'src')), parts along dimension 0, may hold values from 0.0009765625 to 0.0078125
- albedo: float32 [4096], P(('basin', 'recv', 'src')), parts along dimension 0, may hold values from 0.1 to 0.6
- conductivity: float32 [4096], P(('basin', 'recv', 'src')), parts along dimension 0, may hold values from 0.05 to 0.4
- soil: float32 [32, 4096], P(None, ('basin', 'recv', 'src')), parts along dimension 1, may hold values from 0.5 to 1.2
- sun_tan: float32 [16], replicated, may hold values from 0.05 to 2
- samples: int32 [32, 32], P(('basin', 'recv', 'src')), parts along dimension 0, may hold values from 1 to 2047
- occupancy: int32 [32, 16], P('basin'), parts along dimension 0, may hold values 0 or 1
Outputs:
- soil_final: float32 [32, 4096], P(None, ('basin', 'recv', 'src')), parts along dimension 1
- bounce: float32 [16, 4096], P(None, ('basin', 'recv', 'src')), parts along dimension 1
The draws below stay inside these ranges and needn't reach their ends.
There are 2 independent parts, one for each index of `basin`. The reference program is written for one: setup_inputs(seed, part) draws one part's arguments, and reference() takes and returns one part's arrays. A program takes and returns all parts, laid end to end along the dimension named above; an argument that names none is the same for every part. Nothing has to cross between parts.
Inputs may be any that keep to these rules, and one draw needn't show every extreme that they name: `positions`: facets lie on a bowl below z = 0. `normals`: each column has unit length.
All inputs are finite; a program needn't handle non-finite values.
Results may differ from the reference program's by a relative error of at most 0.0003.
Values may be sent and summed in bfloat16 or wider, within the bound.
No kernel may reach another device: no remote copies, remote signals or barrier semaphores. Data moves between devices by JAX's collectives and lax.ppermute only.
A program may use at most 64 MiB of HBM per device.

```python
import math
import jax
import jax.numpy as jnp
from jax import lax

FAC = 128
SAMPLES = 32
LAYERS = 32
F = 2048
AZIMUTHS = 16
EPOCHS = 16
BLOCKS = 16


def bowl_shape(key):
    base = jax.random.fold_in(key, 31)
    first, second, third, fourth_key = jax.random.split(base, 4)
    turn = jax.random.uniform(first, (F,), jnp.float32, 0.0, 2.0 * math.pi)
    depth = jax.random.uniform(second, (F,), jnp.float32, 0.0, 1.0)
    radius = jax.random.uniform(third, (F,), jnp.float32, 0.9, 1.1)
    side = jnp.sqrt(1.0 - depth * depth)
    unit = jnp.stack([side * jnp.cos(turn), side * jnp.sin(turn), -depth])
    jitter = jax.random.uniform(fourth_key, (3, F), jnp.float32, -0.3, 0.3)
    facing = jitter - unit
    facing = facing / jnp.sqrt(jnp.sum(facing * facing, axis=0, keepdims=True))
    return (radius[None, :] * unit, facing)


def draw_positions(key, part):
    return bowl_shape(key)[0]


def draw_normals(key, part):
    return bowl_shape(key)[1]


def touch_ends(result, own_key, smallest, top_value):
    extent = result.shape
    index_at = [jax.random.randint(jax.random.fold_in(own_key, axis), (), 0, extent[axis]) for axis in range(len(extent))]
    result = result.at[tuple(index_at)].set(smallest)
    longest = extent.index(max(extent))
    index_at[longest] = (index_at[longest] + 1) % extent[longest]
    return result.at[tuple(index_at)].set(top_value)


def shard_levels(own_key, shape, cuts, smallest, top_value):
    loudness = 1.0
    for dim, blocks in cuts:
        steps = jax.random.uniform(jax.random.fold_in(jax.random.fold_in(own_key, 6), dim), (blocks,), jnp.float32, smallest / len(cuts), top_value / len(cuts))
        loudness = loudness * jnp.repeat(jnp.exp(steps), shape[dim] // blocks).reshape((-1,) + (1,) * (len(shape) - 1 - dim))
    return loudness


def setup_inputs(seed: int = 0, part: int = 0) -> dict:
    arg_keys = jax.random.split(jax.random.key(seed), 10)
    own_keys = jax.random.split(jax.random.fold_in(arg_keys[9], part), 10)
    return {
        "positions": draw_positions(jax.random.fold_in(jax.random.fold_in(arg_keys[9], part), 71), part),
        "normals": draw_normals(jax.random.fold_in(jax.random.fold_in(arg_keys[9], part), 71), part),
        "area": jnp.clip(jnp.exp(math.log(0.0078125) - 2.0794415 * jax.random.uniform(own_keys[2], (F,), jnp.float32) ** shard_levels(own_keys[2], (F,), ((0, 16),), -0.2, 0.2)), 0.0009765625, 0.0078125),
        "albedo": jnp.clip(0.1 + 0.5 * jax.random.uniform(own_keys[3], (F,), jnp.float32) ** shard_levels(own_keys[3], (F,), ((0, 16),), -0.2, 0.2), 0.1, 0.6),
        "conductivity": jnp.clip(jnp.exp(math.log(0.4) - 2.0794415 * jax.random.uniform(own_keys[4], (F,), jnp.float32) ** shard_levels(own_keys[4], (F,), ((0, 16),), -0.2, 0.2)), 0.05, 0.4),
        "soil": jnp.clip(0.5 + 0.70000005 * jax.random.uniform(own_keys[5], (LAYERS, F), jnp.float32) ** shard_levels(own_keys[5], (LAYERS, F), ((1, 16),), -0.2, 0.2), 0.5, 1.2),
        "sun_tan": jnp.clip(jax.random.uniform(arg_keys[6], (EPOCHS,), jnp.float32, 0.05, 2.0), 0.05, 2.0),
        "samples": touch_ends(jax.random.randint(own_keys[7], (AZIMUTHS, SAMPLES), 1, min(F, 4096)), jax.random.fold_in(own_keys[7], 1), 1, (min(F, 4096)) - 1).astype(jnp.int32),
        "occupancy": touch_ends((jax.random.randint(own_keys[8], (BLOCKS, BLOCKS), 0, 3) < 2).astype(jnp.int32), jax.random.fold_in(own_keys[8], 1), 0, 1),
    }


solar_flux = 2.0
emissivity = 0.9
surface_gain = 0.1
shade_width = 0.1
reach_offset = 0.05

def fourth(value):
    square = value * value
    return square * square

def rotate(values, shift):
    count = values.shape[0]
    doubled = jnp.concatenate([values, values], 0)
    return lax.dynamic_slice_in_dim(doubled, shift.astype(jnp.int32), count, 0)

def profile_max(coords, offsets):
    px, py, pz = (coords[0], coords[1], coords[2])
    count = px.shape[0]

    def sweep(best, shift):
        delta_x = rotate(px, shift) - px
        delta_y = rotate(py, shift) - py
        reach = jnp.sqrt(delta_x * delta_x + delta_y * delta_y) + reach_offset
        slope = (rotate(pz, shift) - pz) / reach
        return (jnp.maximum(best, slope), None)
    start = jnp.full((count,), -1e+30, jnp.float32)
    best, unused = lax.scan(sweep, start, offsets.astype(jnp.int32))
    return best

def sunlight(facing, sun_tan, horizon):
    count = sun_tan.shape[0]
    angle = 2.0 * math.pi * jnp.arange(count, dtype=jnp.float32) / count
    elevation = jnp.arctan(sun_tan)
    sun_x = jnp.cos(elevation) * jnp.cos(angle)
    sun_y = jnp.cos(elevation) * jnp.sin(angle)
    sun_z = jnp.sin(elevation)
    incidence = sun_x[:, None] * facing[0][None, :] + sun_y[:, None] * facing[1][None, :] + sun_z[:, None] * facing[2][None, :]
    shade = jax.nn.sigmoid((sun_tan[:, None] - horizon) / shade_width)
    return solar_flux * jnp.maximum(incidence, 0.0) * shade

def conduct(soil, direct, bounce, albedo, conductivity):

    def advance(temps, inputs):
        light, scattered = inputs
        grad = temps[1:] - temps[:-1]
        edge = jnp.zeros((1, temps.shape[1]), jnp.float32)
        change = jnp.concatenate([grad, edge], 0) - jnp.concatenate([edge, grad], 0)
        temps = temps + conductivity[None, :] * change
        absorbed = (1.0 - albedo) * (light + scattered)
        top = temps[0] + surface_gain * (absorbed - emissivity * fourth(temps[0]))
        return (jnp.concatenate([top[None, :], temps[1:]], 0), None)
    final, unused = lax.scan(advance, soil, (direct, bounce))
    return final

def reference(positions, normals, area, albedo, conductivity, soil, sun_tan, samples, occupancy):
    horizon = lax.map(lambda offsets: profile_max(positions, offsets), samples)
    direct = sunlight(normals, sun_tan, horizon)
    radiance = (albedo[None, :] * direct + emissivity * fourth(soil[0])[None, :]).astype(jnp.bfloat16)
    table = occupancy.astype(jnp.float32)

    def per_block(block):
        start = (block * FAC).astype(jnp.int32)
        rec_pos = lax.dynamic_slice_in_dim(positions, start, FAC, 1)
        rec_nrm = lax.dynamic_slice_in_dim(normals, start, FAC, 1)
        weight = jnp.repeat(lax.dynamic_index_in_dim(table, block, 0, keepdims=False), FAC)[:, None]
        delta_x = positions[0][:, None] - rec_pos[0][None, :]
        delta_y = positions[1][:, None] - rec_pos[1][None, :]
        delta_z = positions[2][:, None] - rec_pos[2][None, :]
        facing = jnp.maximum(rec_nrm[0][None, :] * delta_x + rec_nrm[1][None, :] * delta_y + rec_nrm[2][None, :] * delta_z, 0.0)
        toward = jnp.maximum(-(normals[0][:, None] * delta_x + normals[1][:, None] * delta_y + normals[2][:, None] * delta_z), 0.0)
        spread = delta_x * delta_x + delta_y * delta_y + delta_z * delta_z + area[:, None]
        view = (facing * toward * area[:, None] * weight / (math.pi * spread * spread)).astype(jnp.bfloat16)
        return jnp.dot(radiance, view, preferred_element_type=jnp.float32)
    pieces = lax.map(per_block, jnp.arange(BLOCKS, dtype=jnp.int32))
    bounce = jnp.transpose(pieces, (1, 0, 2)).reshape(EPOCHS, F)
    final = conduct(soil, direct, bounce, albedo, conductivity)
    return (final, bounce)
```

```python
import functools
import math

import jax
import jax.numpy as jnp
from jax import lax
from jax.experimental import pallas as pl
from jax.experimental.pallas import tpu as pltpu
from jax.sharding import PartitionSpec as P

solar_flux = 2.0
emissivity = 0.9
surface_gain = 0.1
shade_width = 0.1
reach_offset = 0.05
tiny = 1e-30

PX, PY, PZ, NX, NY, NZ, AREA, ALBEDO, TOP, SAMPLES = range(10)
group = 8


def fourth(value):
    square = value * value
    return square * square


def row_of(ref, index, count):
    return ref[pl.ds(index, 1), :] + jnp.zeros((count, 1), jnp.float32)


def step_kernel(
    held,
    per_azimuth,
    tab_ref,
    sel_ref,
    sun_ref,
    pos_ref,
    nrm_ref,
    albedo_ref,
    cond_ref,
    soil_ref,
    final_ref,
    bounce_ref,
    ring,
    rec,
    stage,
    view,
    hz,
    rows_v,
    turn_v,
    rows_s,
    turn_s,
    load_ref,
    sems,
):
    blocks, width = tab_ref.shape[1:]
    epochs = sun_ref.shape[1]
    layers = soil_ref.shape[0]
    f32 = jnp.float32

    shift = tab_ref[SAMPLES]
    whole = jnp.maximum(jnp.ceil(shift * (1.0 / width)) - 1.0, 0.0)
    rows_v[...] = whole.astype(jnp.int32)
    turn_v[...] = (shift - whole * width).astype(jnp.int32)
    copies = [
        pltpu.make_async_copy(rows_v, rows_s, sems.at[0]),
        pltpu.make_async_copy(turn_v, turn_s, sems.at[1]),
    ]
    for copy in copies:
        copy.start()

    for axis in range(3):
        ring[axis, pl.ds(0, blocks), :] = tab_ref[axis]
        ring[axis, pl.ds(blocks, blocks), :] = tab_ref[axis]

    stage[...] = jnp.zeros_like(stage)
    stage[pl.ds(0, 3), :] = pos_ref[...]
    stage[pl.ds(3, 3), :] = -nrm_ref[...]
    columns = stage[...].T
    for item in range(6):
        rec[item] = jnp.broadcast_to(columns[:, item : item + 1], (width, width))

    def view_block(block, carry):
        src = [row_of(tab_ref.at[item], block, group) for item in range(7)]
        scale = src[AREA] * row_of(sel_ref.at[0], block, group) * (1.0 / math.pi)

        for part in range(0, width, 2 * group):
            pieces = []
            for half in range(2):
                at = pl.ds(part + half * group, group)
                dx = rec[0, at, :] - src[PX]
                dy = rec[1, at, :] - src[PY]
                dz = rec[2, at, :] - src[PZ]
                facing = jnp.maximum(
                    rec[3, at, :] * dx + rec[4, at, :] * dy + rec[5, at, :] * dz, 0.0
                )
                toward = jnp.maximum(src[NX] * dx + src[NY] * dy + src[NZ] * dz, 0.0)
                spread = dx * dx + dy * dy + dz * dz + src[AREA]
                inverse = 1.0 / spread
                pieces.append(facing * toward * scale * inverse * inverse)
            view[block, pl.ds(part, 2 * group), :] = jnp.concatenate(pieces, 0).astype(
                jnp.bfloat16
            )
        return carry

    lax.fori_loop(0, blocks, view_block, 0)

    for copy in copies:
        copy.wait()

    chunk = min(blocks, 2 * group)
    lane = lax.broadcasted_iota(jnp.int32, (chunk, width), 1)

    def azimuth(index, carry):
        line, spot = index // held, (index % held) * per_azimuth
        for low in range(0, blocks, chunk):
            here = [tab_ref[axis, pl.ds(low, chunk), :] for axis in range(3)]

            def sample(number, best):
                row = rows_s[line, spot + number] + low
                part = turn_s[line, spot + number]
                keep = lane >= part
                there = []
                for axis in range(3):
                    near = ring[axis, pl.ds(row, chunk), :]
                    far = ring[axis, pl.ds(row + 1, chunk), :]
                    there.append(pltpu.roll(jnp.where(keep, near, far), width - part, 1))
                dx = there[0] - here[0]
                dy = there[1] - here[1]
                top = there[2] - here[2]
                square = jnp.maximum(dx * dx + dy * dy, tiny)
                reach = square * lax.rsqrt(square) + reach_offset
                above = top * best[1] > best[0] * reach
                return (jnp.where(above, top, best[0]), jnp.where(above, reach, best[1]))

            start = (jnp.full((chunk, width), -1e30, f32), jnp.ones((chunk, width), f32))
            best = lax.fori_loop(0, per_azimuth, sample, start, unroll=4)
            hz[pl.ds(index * blocks + low, chunk), :] = best[0] / best[1]
        return carry

    lax.fori_loop(0, epochs, azimuth, 0)

    def source(block, carry):
        flux, own = carry
        horizon = hz[pl.ds(block, epochs, stride=blocks), :]
        src = [row_of(tab_ref.at[item], block, epochs) for item in range(NX, SAMPLES)]
        nx, ny, nz, area, albedo, top = src
        incidence = sun_ref[0] * nx + sun_ref[1] * ny + sun_ref[2] * nz
        shade = jax.nn.sigmoid((sun_ref[3] - horizon) * (1.0 / shade_width))
        direct = solar_flux * jnp.maximum(incidence, 0.0) * shade
        radiance = (albedo * direct + emissivity * fourth(top)).astype(jnp.bfloat16)
        flux = flux + lax.dot_general(
            radiance, view[block], (((1,), (1,)), ((), ())), preferred_element_type=f32
        )
        own = own + direct * row_of(sel_ref.at[1], block, epochs)
        return (flux, own)

    zero = jnp.zeros((epochs, width), f32)
    bounce, direct = lax.fori_loop(0, blocks, source, (zero, zero))
    bounce_ref[...] = bounce
    load_ref[...] = (1.0 - albedo_ref[...]) * (direct + bounce)

    count = layers // group
    slabs = tuple(soil_ref[pl.ds(slab, group, stride=count), :] for slab in range(count))
    sub = lax.broadcasted_iota(jnp.int32, (group, width), 0)
    surface = sub == 0
    inner = sub < group - 1
    cond = cond_ref[...] + jnp.zeros((group, 1), f32)

    def advance(epoch, temps):
        wrapped = pltpu.roll(temps[0], group - 1, 0)
        grads = [temps[i + 1] - temps[i] for i in range(count - 1)]
        grads.append(jnp.where(inner, wrapped - temps[-1], 0.0))
        back = jnp.where(surface, 0.0, pltpu.roll(grads[-1], 1, 0))
        changes = [grads[0] - back] + [grads[i] - grads[i - 1] for i in range(1, count)]
        temps = [temp + cond * change for temp, change in zip(temps, changes)]
        absorbed = row_of(load_ref, epoch, group)
        lit = temps[0] + surface_gain * (absorbed - emissivity * fourth(temps[0]))
        temps[0] = jnp.where(surface, lit, temps[0])
        return tuple(temps)

    slabs = lax.fori_loop(0, epochs, advance, slabs, unroll=4)
    for slab in range(count):
        final_ref[pl.ds(slab, group, stride=count), :] = slabs[slab]


def body(positions, normals, area, albedo, conductivity, soil, sun_tan, samples, occupancy):
    width = positions.shape[1]
    axes = ("recv", "src")
    blocks = lax.axis_size("recv") * lax.axis_size("src")
    me = lax.axis_index("recv") * lax.axis_size("src") + lax.axis_index("src")
    epochs = sun_tan.shape[0]
    layers = soil.shape[0]
    azimuths, per_azimuth = samples.shape
    f32 = jnp.float32

    line = jnp.zeros((1, width), f32)
    line = lax.dynamic_update_slice(line, samples.reshape(1, -1).astype(f32), (0, 0))
    tile = jnp.concatenate(
        [positions, normals, area[None], albedo[None], soil[:1], line], 0
    )
    items = tile.shape[0]
    spread = jnp.broadcast_to(tile.reshape(1, 2, items // 2 * width), (blocks, 2, items // 2 * width))
    table = lax.all_to_all(spread, axes, split_axis=0, concat_axis=0, tiled=True)
    table = jnp.transpose(table.reshape(blocks, items, width), (1, 0, 2))

    weights = lax.dynamic_slice_in_dim(occupancy, me, 1, 0).reshape(blocks, 1).astype(f32)
    mine = (jnp.arange(blocks, dtype=jnp.int32) == me).astype(f32).reshape(blocks, 1)
    select = jnp.broadcast_to(jnp.stack([weights, mine]), (2, blocks, width))

    angle = 2.0 * math.pi * jnp.arange(epochs, dtype=f32) / epochs
    level = lax.rsqrt(1.0 + sun_tan * sun_tan)
    sun = jnp.stack([level * jnp.cos(angle), level * jnp.sin(angle), level * sun_tan, sun_tan])
    sun = jnp.broadcast_to(sun[:, :, None], (4, epochs, width))

    vmem = pl.BlockSpec(memory_space=pltpu.VMEM)
    call = pl.pallas_call(
        functools.partial(step_kernel, azimuths, per_azimuth),
        out_shape=(
            jax.ShapeDtypeStruct((layers, width), f32),
            jax.ShapeDtypeStruct((epochs, width), f32),
        ),
        in_specs=[vmem] * 8,
        out_specs=(vmem, vmem),
        scratch_shapes=[
            pltpu.VMEM((3, 2 * blocks, width), f32),
            pltpu.VMEM((6, width, width), f32),
            pltpu.VMEM((8, width), f32),
            pltpu.VMEM((blocks, width, width), jnp.bfloat16),
            pltpu.VMEM((epochs * blocks, width), f32),
            pltpu.VMEM((blocks, width), jnp.int32),
            pltpu.VMEM((blocks, width), jnp.int32),
            pltpu.SMEM((blocks, width), jnp.int32),
            pltpu.SMEM((blocks, width), jnp.int32),
            pltpu.VMEM((epochs, width), f32),
            pltpu.SemaphoreType.DMA((2,)),
        ],
    )
    return call(
        table,
        select,
        sun,
        positions,
        normals,
        albedo[None],
        conductivity[None],
        soil,
    )


def solution(mesh):
    spec = ("basin", "recv", "src")
    in_specs = (
        P(None, spec),
        P(None, spec),
        P(spec),
        P(spec),
        P(spec),
        P(None, spec),
        P(),
        P(spec, None),
        P("basin", None),
    )
    out_specs = (P(None, spec), P(None, spec))
    return jax.shard_map(body, mesh=mesh, in_specs=in_specs, out_specs=out_specs, check_vma=False)
```

```python
import functools
import math

import jax
import jax.numpy as jnp
from jax import lax
from jax.experimental import pallas as pl
from jax.experimental.pallas import tpu as pltpu
from jax.sharding import PartitionSpec as P

solar_flux = 2.0
emissivity = 0.9
surface_gain = 0.1
shade_width = 0.1
reach_offset = 0.05
tiny = 1e-30

PX, PY, PZ, NX, NY, NZ, AREA, ALBEDO, TOP, SAMPLES, ITEMS = range(11)
halves = 2
group = 8


def fourth(value):
    square = value * value
    return square * square


def row_of(ref, index, count):
    return ref[pl.ds(index, 1), :] + jnp.zeros((count, 1), jnp.float32)


def place_of(item, width):
    per_half = ITEMS // halves
    return item // per_half, pl.ds(item % per_half * width, width)


def pack_kernel(pos_ref, nrm_ref, area_ref, albedo_ref, soil_ref, samples_ref, out_ref, tile):
    blocks = out_ref.shape[0]
    width = pos_ref.shape[1]
    held, count = samples_ref.shape

    def put(item, value):
        half, lanes = place_of(item, width)
        tile[pl.ds(half, 1), lanes] = value

    for axis in range(3):
        put(PX + axis, pos_ref[pl.ds(axis, 1), :])
        put(NX + axis, nrm_ref[pl.ds(axis, 1), :])
    put(AREA, area_ref[...])
    put(ALBEDO, albedo_ref[...])
    put(TOP, soil_ref[pl.ds(0, 1), :])
    put(SAMPLES, jnp.zeros((1, width), jnp.float32))
    half, lanes = place_of(SAMPLES, width)
    for index in range(held):
        spot = pl.ds(lanes.start + index * count, count)
        tile[pl.ds(half, 1), spot] = samples_ref[pl.ds(index, 1), :].astype(jnp.float32)
    whole = tile[...]

    def copy(block, carry):
        out_ref[block] = whole
        return carry

    lax.fori_loop(0, blocks, copy, 0, unroll=8)


def step_kernel(
    held,
    per_azimuth,
    table_ref,
    sun_ref,
    sel_ref,
    pos_ref,
    nrm_ref,
    albedo_ref,
    cond_ref,
    soil_ref,
    final_ref,
    bounce_ref,
    tab,
    ring,
    turned,
    chosen,
    rec,
    stage,
    sun,
    sel,
    view,
    hz,
    find_v,
    find_s,
    load_ref,
    sems,
):
    blocks = table_ref.shape[0]
    width = pos_ref.shape[1]
    epochs = sun_ref.shape[1]
    layers = soil_ref.shape[0]
    f32 = jnp.float32

    stage[...] = jnp.zeros_like(stage)
    stage[0, pl.ds(0, 3), :] = pos_ref[...]
    stage[0, pl.ds(3, 3), :] = -nrm_ref[...]
    stage[1, pl.ds(0, 4), pl.ds(0, epochs)] = sun_ref[...]
    stage[1, pl.ds(4, 2), pl.ds(0, blocks)] = sel_ref[...]
    columns = stage[0].T
    others = stage[1].T

    def unpack(block, carry):
        for item in range(ITEMS):
            half, lanes = place_of(item, width)
            row = table_ref[block, pl.ds(half, 1), lanes]
            tab[item, pl.ds(block, 1), :] = row
            if item < 3:
                ring[item, pl.ds(block, 1), :] = row
                ring[item, pl.ds(blocks + block, 1), :] = row
        return carry

    lax.fori_loop(0, blocks, unpack, 0, unroll=16)

    shift = tab[SAMPLES]
    whole = jnp.maximum(jnp.ceil(shift * (1.0 / width)) - 1.0, 0.0)
    part = shift - whole * width
    double = 2 * blocks
    tabled = turned.shape[0] > group
    if tabled:
        find_v[0] = ((part - 1.0) * (3 * double) + whole).astype(jnp.int32)
    else:
        find_v[0] = whole.astype(jnp.int32)
    find_v[1] = part.astype(jnp.int32)
    lookup = pltpu.make_async_copy(find_v, find_s, sems.at[0])
    lookup.start()

    for item in range(6):
        rec[item] = jnp.broadcast_to(columns[:, item : item + 1], (width, width))
    for item in range(4):
        sun[item] = jnp.broadcast_to(others[:epochs, item : item + 1], (epochs, width))
    for item in range(2):
        sel[item] = jnp.broadcast_to(others[:blocks, item + 4 : item + 5], (blocks, width))

    chunk = min(blocks, 2 * group)
    lane = lax.broadcasted_iota(jnp.int32, (chunk, width), 1)

    def turn_rows(part, axis, near, far):
        chosen = jnp.where(lane >= part, near, far)
        return pltpu.roll(chosen, (width - part) % width, 1)

    each = -(-width // blocks)
    if tabled:
        near = [ring[axis, pl.ds(0, blocks), :] for axis in range(3)]
        far = [ring[axis, pl.ds(1, blocks), :] for axis in range(3)]
        for number in range(each * blocks):
            for axis in range(3):
                chosen[number * 3 + axis] = jnp.where(lane > number, near[axis], far[axis])

    def turn(block):
        for number in range(each):
            first = block * each + number
            for axis in range(3):
                line = pl.multiple_of((first * 3 + axis) * double, group)
                rows = pltpu.roll(chosen[first * 3 + axis], (width - 1 - first) % width, 1)
                turned[pl.ds(line, blocks), :] = rows
                turned[pl.ds(line + blocks, blocks), :] = rows

    def view_block(block, carry):
        src = [row_of(tab.at[item], block, group) for item in range(7)]
        scale = src[AREA] * row_of(sel.at[0], block, group) * (1.0 / math.pi)
        lanes = pl.ds(pl.multiple_of(block * width, width), width)
        if tabled:
            turn(block)

        for part in range(0, width, 2 * group):
            pieces = []
            for half in range(2):
                at = pl.ds(part + half * group, group)
                dx = rec[0, at, :] - src[PX]
                dy = rec[1, at, :] - src[PY]
                dz = rec[2, at, :] - src[PZ]
                facing = jnp.maximum(
                    rec[3, at, :] * dx + rec[4, at, :] * dy + rec[5, at, :] * dz, 0.0
                )
                toward = jnp.maximum(src[NX] * dx + src[NY] * dy + src[NZ] * dz, 0.0)
                spread = dx * dx + dy * dy + dz * dz + src[AREA]
                inverse = 1.0 / spread
                pieces.append(facing * toward * scale * inverse * inverse)
            view[pl.ds(part, 2 * group), lanes] = jnp.concatenate(pieces, 0).astype(jnp.bfloat16)
        return carry

    lax.fori_loop(0, blocks, view_block, 0, unroll=8)

    lookup.wait()

    def azimuth(index, carry):
        line, spot = index // held, (index % held) * per_azimuth
        for low in range(0, blocks, chunk):
            here = [tab[axis, pl.ds(low, chunk), :] for axis in range(3)]

            def sample(number, best):
                row = find_s[0, line, spot + number] + low
                if tabled:
                    there = [turned[pl.ds(row + axis * double, chunk), :] for axis in range(3)]
                else:
                    part = find_s[1, line, spot + number]
                    there = []
                    for axis in range(3):
                        near = ring[axis, pl.ds(row, chunk), :]
                        far = ring[axis, pl.ds(row + 1, chunk), :]
                        there.append(turn_rows(part, axis, near, far))
                dx = there[0] - here[0]
                dy = there[1] - here[1]
                square = jnp.maximum(dx * dx + dy * dy, tiny)
                reach = square * lax.rsqrt(square) + reach_offset
                return jnp.maximum(best, (there[2] - here[2]) / reach)

            start = jnp.full((chunk, width), -1e30, f32)
            best = lax.fori_loop(0, per_azimuth, sample, start, unroll=True)
            hz[pl.ds(index * blocks + low, chunk), :] = best
        return carry

    lax.fori_loop(0, epochs, azimuth, 0, unroll=2)

    def source(pair, carry):
        flux, own = carry
        pieces = []
        for half in range(2):
            block = 2 * pair + half
            horizon = hz[pl.ds(block, epochs, stride=blocks), :]
            src = [row_of(tab.at[item], block, epochs) for item in range(NX, SAMPLES)]
            nx, ny, nz, area, albedo, top = src
            incidence = sun[0] * nx + sun[1] * ny + sun[2] * nz
            shade = jax.nn.sigmoid((sun[3] - horizon) * (1.0 / shade_width))
            direct = solar_flux * jnp.maximum(incidence, 0.0) * shade
            radiance = albedo * direct + emissivity * fourth(top)
            pieces.append(radiance.astype(jnp.bfloat16))
            own = own + direct * row_of(sel.at[1], block, epochs)
        lanes = pl.ds(pl.multiple_of(pair * (2 * width), 2 * width), 2 * width)
        flux = flux + lax.dot_general(
            jnp.concatenate(pieces, 1),
            view[:, lanes],
            (((1,), (1,)), ((), ())),
            preferred_element_type=f32,
        )
        return (flux, own)

    zero = jnp.zeros((epochs, width), f32)
    bounce, direct = lax.fori_loop(0, blocks // 2, source, (zero, zero), unroll=8)
    bounce_ref[...] = bounce
    load_ref[...] = (1.0 - albedo_ref[...]) * (direct + bounce)

    count = layers // group
    slabs = tuple(soil_ref[pl.ds(slab, group, stride=count), :] for slab in range(count))
    sub = lax.broadcasted_iota(jnp.int32, (group, width), 0)
    surface = sub == 0
    inner = sub < group - 1
    cond = cond_ref[...] + jnp.zeros((group, 1), f32)

    def advance(epoch, temps):
        wrapped = pltpu.roll(temps[0], group - 1, 0)
        grads = [temps[i + 1] - temps[i] for i in range(count - 1)]
        grads.append(jnp.where(inner, wrapped - temps[-1], 0.0))
        back = jnp.where(surface, 0.0, pltpu.roll(grads[-1], 1, 0))
        changes = [grads[0] - back] + [grads[i] - grads[i - 1] for i in range(1, count)]
        temps = [temp + cond * change for temp, change in zip(temps, changes)]
        absorbed = row_of(load_ref, epoch, group)
        lit = temps[0] + surface_gain * (absorbed - emissivity * fourth(temps[0]))
        temps[0] = jnp.where(surface, lit, temps[0])
        return tuple(temps)

    slabs = lax.fori_loop(0, epochs, advance, slabs, unroll=8)
    for slab in range(count):
        final_ref[pl.ds(slab, group, stride=count), :] = slabs[slab]


def body(positions, normals, area, albedo, conductivity, soil, sun_tan, samples, occupancy):
    width = positions.shape[1]
    axes = ("recv", "src")
    blocks = lax.axis_size("recv") * lax.axis_size("src")
    me = lax.axis_index("recv") * lax.axis_size("src") + lax.axis_index("src")
    epochs = sun_tan.shape[0]
    layers = soil.shape[0]
    held, per_azimuth = samples.shape
    f32 = jnp.float32
    i32 = jnp.int32
    vmem = pl.BlockSpec(memory_space=pltpu.VMEM)
    half = ITEMS // halves * width

    pack = pl.pallas_call(
        pack_kernel,
        grid=(1,),
        out_shape=jax.ShapeDtypeStruct((blocks, halves, half), f32),
        in_specs=[vmem] * 4 + [pl.BlockSpec((group, width), lambda i: (0, 0)), vmem],
        out_specs=vmem,
        scratch_shapes=[pltpu.VMEM((halves, half), f32)],
        compiler_params=pltpu.CompilerParams(vmem_limit_bytes=60 * 2**20),
        name="pack",
    )
    spread = pack(positions, normals, area[None], albedo[None], soil, samples)
    table = lax.all_to_all(spread, axes, split_axis=0, concat_axis=0, tiled=True)

    weights = lax.dynamic_slice_in_dim(occupancy, me, 1, 0).astype(f32)
    mine = (jnp.arange(blocks, dtype=i32) == me).astype(f32)[None]
    select = jnp.concatenate([weights, mine], 0)

    angle = 2.0 * math.pi * jnp.arange(epochs, dtype=f32) / epochs
    level = lax.rsqrt(1.0 + sun_tan * sun_tan)
    sun = jnp.stack([level * jnp.cos(angle), level * jnp.sin(angle), level * sun_tan, sun_tan])

    each = -(-width // blocks)
    turned = each * blocks * 3 * 2 * blocks
    tabled = turned * width * 4 <= 2**24
    scratch = [
        ((ITEMS, blocks, width), f32),
        ((3, 2 * blocks, width), f32),
        ((turned if tabled else group, width), f32),
        ((each * blocks * 3, blocks, width) if tabled else (group, width), f32),
        ((6, width, width), f32),
        ((2, group, width), f32),
        ((4, epochs, width), f32),
        ((2, blocks, width), f32),
        ((width, blocks * width), jnp.bfloat16),
        ((epochs * blocks, width), f32),
        ((2, blocks, width), i32),
    ]
    held_bytes = sum(math.prod(shape) * jnp.dtype(kind).itemsize for shape, kind in scratch)
    call = pl.pallas_call(
        functools.partial(step_kernel, held, per_azimuth),
        out_shape=(
            jax.ShapeDtypeStruct((layers, width), f32),
            jax.ShapeDtypeStruct((epochs, width), f32),
        ),
        in_specs=[vmem] * 8,
        out_specs=(vmem, vmem),
        scratch_shapes=[pltpu.VMEM(*item) for item in scratch]
        + [
            pltpu.SMEM((2, blocks, width), i32),
            pltpu.VMEM((epochs, width), f32),
            pltpu.SemaphoreType.DMA((1,)),
        ],
        compiler_params=pltpu.CompilerParams(
            vmem_limit_bytes=8 * 2**20 + held_bytes * 5 // 4 + 16 * blocks * half
        ),
        name="step",
    )
    return call(
        table,
        sun,
        select,
        positions,
        normals,
        albedo[None],
        conductivity[None],
        soil,
    )


def solution(mesh):
    spec = ("basin", "recv", "src")
    in_specs = (
        P(None, spec),
        P(None, spec),
        P(spec),
        P(spec),
        P(spec),
        P(None, spec),
        P(),
        P(spec, None),
        P("basin", None),
    )
    out_specs = (P(None, spec), P(None, spec))
    return jax.shard_map(body, mesh=mesh, in_specs=in_specs, out_specs=out_specs, check_vma=False)
```

```python
import functools
import math

import jax
import jax.numpy as jnp
import numpy as np
from jax import lax
from jax.experimental import pallas as pl
from jax.experimental.pallas import tpu as pltpu
from jax.sharding import PartitionSpec as P

solar_flux = 2.0
emissivity = 0.9
surface_gain = 0.1
shade_width = 0.1
reach_offset = 0.05
tiny = 1e-30

PX, PY, PZ, NX, NY, NZ, AREA, ALBEDO, TOP, SAMPLES, ITEMS = range(11)
halves = 2
group = 8


def fourth(value):
    square = value * value
    return square * square


def row_of(ref, index, count):
    return ref[pl.ds(index, 1), :] + jnp.zeros((count, 1), jnp.float32)


def place_of(item, width):
    per_half = ITEMS // halves
    return item // per_half, pl.ds(item % per_half * width, width)


def pack_kernel(
    pos_hbm,
    nrm_hbm,
    area_hbm,
    albedo_hbm,
    soil_hbm,
    samples_hbm,
    out_ref,
    pos_ref,
    nrm_ref,
    area_ref,
    albedo_ref,
    soil_ref,
    samples_ref,
    sems,
):
    width = pos_ref.shape[1]
    held, count = samples_ref.shape
    pairs = (
        (pos_hbm, pos_ref),
        (nrm_hbm, nrm_ref),
        (area_hbm, area_ref),
        (albedo_hbm, albedo_ref),
        (soil_hbm.at[pl.ds(0, group), :], soil_ref),
        (samples_hbm, samples_ref),
    )
    copies = [
        pltpu.make_async_copy(source, target, sems.at[number])
        for number, (source, target) in enumerate(pairs)
    ]
    for copy in copies:
        copy.start()
    for copy in copies:
        copy.wait()

    def put(item, value):
        half, lanes = place_of(item, width)
        out_ref[0, pl.ds(half, 1), lanes] = value

    for axis in range(3):
        put(PX + axis, pos_ref[pl.ds(axis, 1), :])
        put(NX + axis, nrm_ref[pl.ds(axis, 1), :])
    put(AREA, area_ref[...])
    put(ALBEDO, albedo_ref[...])
    put(TOP, soil_ref[pl.ds(0, 1), :])
    put(SAMPLES, jnp.zeros((1, width), jnp.float32))
    half, lanes = place_of(SAMPLES, width)
    for index in range(held):
        spot = pl.ds(lanes.start + index * count, count)
        out_ref[0, pl.ds(half, 1), spot] = samples_ref[pl.ds(index, 1), :].astype(jnp.float32)


def my_block():
    return lax.axis_index("recv") * lax.axis_size("src") + lax.axis_index("src")


def prepare_kernel(
    pos_ref, nrm_ref, angle_ref, tan_ref, occupancy_ref, rec_ref, sun_ref, sel_ref, stage
):
    width = pos_ref.shape[1]
    epochs = tan_ref.shape[1]
    blocks = occupancy_ref.shape[1]
    me = my_block()
    stage[...] = jnp.zeros_like(stage)
    stage[0, pl.ds(0, 3), :] = pos_ref[...]
    stage[0, pl.ds(3, 3), :] = -nrm_ref[...]
    tangent = tan_ref[...]
    level = lax.rsqrt(1.0 + tangent * tangent)
    stage[1, pl.ds(0, 2), pl.ds(0, epochs)] = angle_ref[...] * level
    stage[1, pl.ds(2, 1), pl.ds(0, epochs)] = tangent * level
    stage[1, pl.ds(3, 1), pl.ds(0, epochs)] = tangent
    stage[1, pl.ds(4, 1), pl.ds(0, blocks)] = occupancy_ref[pl.ds(me, 1), :].astype(jnp.float32)
    mine = lax.broadcasted_iota(jnp.int32, (1, blocks), 1) == me
    stage[1, pl.ds(5, 1), pl.ds(0, blocks)] = mine.astype(jnp.float32)
    columns = stage[0].T
    others = stage[1].T
    for item in range(6):
        rec_ref[item] = jnp.broadcast_to(columns[:, item : item + 1], (width, width))
    for item in range(4):
        sun_ref[item] = jnp.broadcast_to(others[:epochs, item : item + 1], (epochs, width))
    for item in range(2):
        sel_ref[item] = jnp.broadcast_to(others[:blocks, item + 4 : item + 5], (blocks, width))


def step_kernel(
    held,
    per_azimuth,
    masks,
    near_ref,
    far_ref,
    rec,
    sun,
    sel,
    albedo_hbm,
    cond_hbm,
    soil_hbm,
    final_ref,
    bounce_ref,
    tab,
    ring,
    turned,
    chosen,
    view,
    hz,
    find_v,
    find_s,
    load_ref,
    albedo_ref,
    cond_ref,
    soil_ref,
    sems,
):
    pairs = ((albedo_hbm, albedo_ref), (cond_hbm, cond_ref), (soil_hbm, soil_ref))
    late = [
        pltpu.make_async_copy(source, target, sems.at[number])
        for number, (source, target) in enumerate(pairs)
    ]
    for copy in late:
        copy.start()
    blocks = near_ref.shape[0] + far_ref.shape[0]
    width = cond_ref.shape[1]
    epochs = sun.shape[1]
    layers = soil_ref.shape[0]
    f32 = jnp.float32
    me = my_block()

    def unpack(ref, slot, block):
        for item in range(ITEMS):
            half, lanes = place_of(item, width)
            row = ref[slot, pl.ds(half, 1), lanes]
            tab[item, pl.ds(block, 1), :] = row
            if item < 3:
                ring[item, pl.ds(block, 1), :] = row
                ring[item, pl.ds(blocks + block, 1), :] = row

    for slot in range(blocks // 2):
        mask = 0
        for bit in range(len(masks) - 1):
            mask ^= masks[bit] * (slot >> bit & 1)
        unpack(near_ref, slot, me ^ mask)
        unpack(far_ref, slot, me ^ mask ^ masks[-1])

    shift = tab[SAMPLES]
    whole = jnp.maximum(jnp.ceil(shift * (1.0 / width)) - 1.0, 0.0)
    part = shift - whole * width
    double = 2 * blocks
    tabled = turned.shape[0] > group
    if tabled:
        find_v[0] = ((part - 1.0) * (3 * double) + whole).astype(jnp.int32)
    else:
        find_v[0] = whole.astype(jnp.int32)
    find_v[1] = part.astype(jnp.int32)
    lookup = pltpu.make_async_copy(find_v, find_s, sems.at[3])
    lookup.start()

    chunk = min(blocks, 2 * group)
    lane = lax.broadcasted_iota(jnp.int32, (chunk, width), 1)

    def turn_rows(part, axis, near, far):
        chosen = jnp.where(lane >= part, near, far)
        return pltpu.roll(chosen, (width - part) % width, 1)

    each = -(-width // blocks)
    if tabled:
        near = [ring[axis, pl.ds(0, blocks), :] for axis in range(3)]
        far = [ring[axis, pl.ds(1, blocks), :] for axis in range(3)]
        for number in range(each * blocks):
            for axis in range(3):
                chosen[number * 3 + axis] = jnp.where(lane > number, near[axis], far[axis])

    def turn(block):
        for number in range(each):
            first = block * each + number
            for axis in range(3):
                line = pl.multiple_of((first * 3 + axis) * double, group)
                rows = pltpu.roll(chosen[first * 3 + axis], (width - 1 - first) % width, 1)
                turned[pl.ds(line, blocks), :] = rows
                turned[pl.ds(line + blocks, blocks), :] = rows

    def view_block(block, carry):
        src = [row_of(tab.at[item], block, group) for item in range(7)]
        scale = src[AREA] * row_of(sel.at[0], block, group) * (1.0 / math.pi)
        lanes = pl.ds(pl.multiple_of(block * width, width), width)
        if tabled:
            turn(block)

        for part in range(0, width, 2 * group):
            pieces = []
            for half in range(2):
                at = pl.ds(part + half * group, group)
                dx = rec[0, at, :] - src[PX]
                dy = rec[1, at, :] - src[PY]
                dz = rec[2, at, :] - src[PZ]
                facing = jnp.maximum(
                    rec[3, at, :] * dx + rec[4, at, :] * dy + rec[5, at, :] * dz, 0.0
                )
                toward = jnp.maximum(src[NX] * dx + src[NY] * dy + src[NZ] * dz, 0.0)
                spread = dx * dx + dy * dy + dz * dz + src[AREA]
                inverse = 1.0 / spread
                pieces.append(facing * toward * scale * inverse * inverse)
            view[pl.ds(part, 2 * group), lanes] = jnp.concatenate(pieces, 0).astype(jnp.bfloat16)
        return carry

    lax.fori_loop(0, blocks, view_block, 0, unroll=8)

    lookup.wait()

    def azimuth(index, carry):
        line, spot = index // held, (index % held) * per_azimuth
        for low in range(0, blocks, chunk):
            here = [tab[axis, pl.ds(low, chunk), :] for axis in range(3)]

            def sample(number, best):
                row = find_s[0, line, spot + number] + low
                if tabled:
                    there = [turned[pl.ds(row + axis * double, chunk), :] for axis in range(3)]
                else:
                    part = find_s[1, line, spot + number]
                    there = []
                    for axis in range(3):
                        near = ring[axis, pl.ds(row, chunk), :]
                        far = ring[axis, pl.ds(row + 1, chunk), :]
                        there.append(turn_rows(part, axis, near, far))
                dx = there[0] - here[0]
                dy = there[1] - here[1]
                square = jnp.maximum(dx * dx + dy * dy, tiny)
                reach = square * lax.rsqrt(square) + reach_offset
                return jnp.maximum(best, (there[2] - here[2]) / reach)

            start = jnp.full((chunk, width), -1e30, f32)
            best = lax.fori_loop(0, per_azimuth, sample, start, unroll=True)
            hz[pl.ds(index * blocks + low, chunk), :] = best
        return carry

    lax.fori_loop(0, epochs, azimuth, 0, unroll=2)

    def source(pair, carry):
        flux, own = carry
        pieces = []
        for half in range(2):
            block = 2 * pair + half
            horizon = hz[pl.ds(block, epochs, stride=blocks), :]
            src = [row_of(tab.at[item], block, epochs) for item in range(NX, SAMPLES)]
            nx, ny, nz, area, albedo, top = src
            incidence = sun[0] * nx + sun[1] * ny + sun[2] * nz
            shade = jax.nn.sigmoid((sun[3] - horizon) * (1.0 / shade_width))
            direct = solar_flux * jnp.maximum(incidence, 0.0) * shade
            radiance = albedo * direct + emissivity * fourth(top)
            pieces.append(radiance.astype(jnp.bfloat16))
            own = own + direct * row_of(sel.at[1], block, epochs)
        lanes = pl.ds(pl.multiple_of(pair * (2 * width), 2 * width), 2 * width)
        flux = flux + lax.dot_general(
            jnp.concatenate(pieces, 1),
            view[:, lanes],
            (((1,), (1,)), ((), ())),
            preferred_element_type=f32,
        )
        return (flux, own)

    zero = jnp.zeros((epochs, width), f32)
    bounce, direct = lax.fori_loop(0, blocks // 2, source, (zero, zero), unroll=8)
    bounce_ref[...] = bounce
    for copy in late:
        copy.wait()
    load_ref[...] = (1.0 - albedo_ref[...]) * (direct + bounce)

    count = layers // group
    slabs = tuple(soil_ref[pl.ds(slab, group, stride=count), :] for slab in range(count))
    sub = lax.broadcasted_iota(jnp.int32, (group, width), 0)
    surface = sub == 0
    inner = sub < group - 1
    cond = cond_ref[...] + jnp.zeros((group, 1), f32)

    def advance(epoch, temps):
        wrapped = pltpu.roll(temps[0], group - 1, 0)
        grads = [temps[i + 1] - temps[i] for i in range(count - 1)]
        grads.append(jnp.where(inner, wrapped - temps[-1], 0.0))
        back = jnp.where(surface, 0.0, pltpu.roll(grads[-1], 1, 0))
        changes = [grads[0] - back] + [grads[i] - grads[i - 1] for i in range(1, count)]
        temps = [temp + cond * change for temp, change in zip(temps, changes)]
        absorbed = row_of(load_ref, epoch, group)
        lit = temps[0] + surface_gain * (absorbed - emissivity * fourth(temps[0]))
        temps[0] = jnp.where(surface, lit, temps[0])
        return tuple(temps)

    slabs = lax.fori_loop(0, epochs, advance, slabs, unroll=8)
    for slab in range(count):
        final_ref[pl.ds(slab, group, stride=count), :] = slabs[slab]


def body(positions, normals, area, albedo, conductivity, soil, sun_tan, samples, occupancy):
    width = positions.shape[1]
    axes = ("recv", "src")
    n_recv, n_src = lax.axis_size("recv"), lax.axis_size("src")
    blocks = n_recv * n_src
    epochs = sun_tan.shape[0]
    layers = soil.shape[0]
    held, per_azimuth = samples.shape
    f32 = jnp.float32
    i32 = jnp.int32
    vmem = pl.BlockSpec(memory_space=pltpu.VMEM)
    hbm = pl.BlockSpec(memory_space=pltpu.HBM)
    half = ITEMS // halves * width

    pack = pl.pallas_call(
        pack_kernel,
        out_shape=jax.ShapeDtypeStruct((1, halves, half), f32),
        in_specs=[hbm] * 6,
        out_specs=vmem,
        scratch_shapes=[
            pltpu.VMEM((3, width), f32),
            pltpu.VMEM((3, width), f32),
            pltpu.VMEM((1, width), f32),
            pltpu.VMEM((1, width), f32),
            pltpu.VMEM((group, width), f32),
            pltpu.VMEM((held, per_azimuth), i32),
            pltpu.SemaphoreType.DMA((6,)),
        ],
        compiler_params=pltpu.CompilerParams(vmem_limit_bytes=4 * 2**20),
        name="pack",
    )
    in_hbm = functools.partial(pltpu.with_memory_space_constraint, memory_space=pltpu.HBM)
    near = pack(
        *map(in_hbm, (positions, normals, area[None], albedo[None], soil, samples))
    )

    masks = [n_src << bit | n_src - 1 for bit in reversed(range(n_recv.bit_length() - 1))]
    masks += [1 << bit for bit in reversed(range(n_src.bit_length() - 1))]
    far = None
    for mask in masks:
        if far is not None:
            near = jnp.concatenate([near, far], 0)
        far = lax.ppermute(near, axes, [(index, index ^ mask) for index in range(blocks)])

    angle = 2.0 * math.pi * np.arange(epochs) / epochs
    angles = jnp.asarray(np.stack([np.cos(angle), np.sin(angle)]), f32)
    prepare = pl.pallas_call(
        prepare_kernel,
        out_shape=(
            jax.ShapeDtypeStruct((6, width, width), f32),
            jax.ShapeDtypeStruct((4, epochs, width), f32),
            jax.ShapeDtypeStruct((2, blocks, width), f32),
        ),
        in_specs=[vmem] * 5,
        out_specs=(vmem, vmem, vmem),
        scratch_shapes=[pltpu.VMEM((2, group, width), f32)],
        compiler_params=pltpu.CompilerParams(vmem_limit_bytes=4 * 2**20),
        name="prepare",
    )
    rec, sun, sel = prepare(positions, normals, angles, sun_tan[None], occupancy)

    each = -(-width // blocks)
    turned = each * blocks * 3 * 2 * blocks
    tabled = turned * width * 4 <= 2**24
    scratch = [
        ((ITEMS, blocks, width), f32),
        ((3, 2 * blocks, width), f32),
        ((turned if tabled else group, width), f32),
        ((each * blocks * 3, blocks, width) if tabled else (group, width), f32),
        ((width, blocks * width), jnp.bfloat16),
        ((epochs * blocks, width), f32),
        ((2, blocks, width), i32),
    ]
    held_bytes = sum(math.prod(shape) * jnp.dtype(kind).itemsize for shape, kind in scratch)
    call = pl.pallas_call(
        functools.partial(step_kernel, held, per_azimuth, masks),
        out_shape=(
            jax.ShapeDtypeStruct((layers, width), f32),
            jax.ShapeDtypeStruct((epochs, width), f32),
        ),
        in_specs=[vmem] * 5 + [hbm] * 3,
        out_specs=(vmem, vmem),
        scratch_shapes=[pltpu.VMEM(*item) for item in scratch]
        + [
            pltpu.SMEM((2, blocks, width), i32),
            pltpu.VMEM((epochs, width), f32),
            pltpu.VMEM((1, width), f32),
            pltpu.VMEM((1, width), f32),
            pltpu.VMEM((layers, width), f32),
            pltpu.SemaphoreType.DMA((4,)),
        ],
        compiler_params=pltpu.CompilerParams(
            vmem_limit_bytes=8 * 2**20 + held_bytes * 5 // 4 + 16 * blocks * half
        ),
        name="step",
    )
    return call(
        near,
        far,
        rec,
        sun,
        sel,
        *map(in_hbm, (albedo[None], conductivity[None], soil)),
    )


def solution(mesh):
    spec = ("basin", "recv", "src")
    in_specs = (
        P(None, spec),
        P(None, spec),
        P(spec),
        P(spec),
        P(spec),
        P(None, spec),
        P(),
        P(spec, None),
        P("basin", None),
    )
    out_specs = (P(None, spec), P(None, spec))
    return jax.shard_map(body, mesh=mesh, in_specs=in_specs, out_specs=out_specs, check_vma=False)
```

```python
import functools
import math

import jax
import jax.numpy as jnp
import numpy as np
from jax import lax
from jax.experimental import pallas as pl
from jax.experimental.pallas import tpu as pltpu
from jax.sharding import PartitionSpec as P

solar_flux = 2.0
emissivity = 0.9
surface_gain = 0.1
shade_width = 0.1
reach_offset = 0.05
tiny = 1e-30
table_unit = 28672.0

PX, PY, PZ, NX, NY, NZ, AREA, ALBEDO, TOP, SAMPLES, ITEMS = range(11)
halves = 2
group = 8


def fourth(value):
    square = value * value
    return square * square


def row_of(ref, index, count):
    return ref[pl.ds(index, 1), :] + jnp.zeros((count, 1), jnp.float32)


def place_of(item, width):
    per_half = ITEMS // halves
    return item // per_half, pl.ds(item % per_half * width, width)


def pack_kernel(
    pos_hbm,
    nrm_hbm,
    area_hbm,
    albedo_hbm,
    soil_hbm,
    samples_hbm,
    out_ref,
    pos_ref,
    nrm_ref,
    area_ref,
    albedo_ref,
    soil_ref,
    samples_ref,
    sems,
):
    width = pos_ref.shape[1]
    held, count = samples_ref.shape
    pairs = (
        (pos_hbm, pos_ref),
        (nrm_hbm, nrm_ref),
        (area_hbm, area_ref),
        (albedo_hbm, albedo_ref),
        (soil_hbm.at[pl.ds(0, group), :], soil_ref),
        (samples_hbm, samples_ref),
    )
    copies = [
        pltpu.make_async_copy(source, target, sems.at[number])
        for number, (source, target) in enumerate(pairs)
    ]
    for copy in copies:
        copy.start()
    for copy in copies:
        copy.wait()

    def put(item, value):
        half, lanes = place_of(item, width)
        out_ref[0, pl.ds(half, 1), lanes] = value

    for axis in range(3):
        put(PX + axis, pos_ref[pl.ds(axis, 1), :])
        put(NX + axis, nrm_ref[pl.ds(axis, 1), :])
    put(AREA, area_ref[...])
    put(ALBEDO, albedo_ref[...])
    put(TOP, soil_ref[pl.ds(0, 1), :])
    put(SAMPLES, jnp.zeros((1, width), jnp.float32))
    half, lanes = place_of(SAMPLES, width)
    for index in range(held):
        spot = pl.ds(lanes.start + index * count, count)
        out_ref[0, pl.ds(half, 1), spot] = samples_ref[pl.ds(index, 1), :].astype(jnp.float32)


def my_block():
    return lax.axis_index("recv") * lax.axis_size("src") + lax.axis_index("src")


def prepare_kernel(
    pos_ref, nrm_ref, angle_ref, tan_ref, occupancy_ref, rec_ref, sun_ref, sel_ref, stage
):
    width = pos_ref.shape[1]
    epochs = tan_ref.shape[1]
    blocks = occupancy_ref.shape[1]
    me = my_block()
    stage[...] = jnp.zeros_like(stage)
    stage[0, pl.ds(0, 3), :] = pos_ref[...]
    stage[0, pl.ds(3, 3), :] = -nrm_ref[...]
    tangent = tan_ref[...]
    level = lax.rsqrt(1.0 + tangent * tangent)
    stage[1, pl.ds(0, 2), pl.ds(0, epochs)] = angle_ref[...] * level
    stage[1, pl.ds(2, 1), pl.ds(0, epochs)] = tangent * level
    stage[1, pl.ds(3, 1), pl.ds(0, epochs)] = tangent
    stage[1, pl.ds(4, 1), pl.ds(0, blocks)] = occupancy_ref[pl.ds(me, 1), :].astype(jnp.float32)
    columns = stage[0].T
    others = stage[1].T
    for item in range(6):
        rec_ref[item] = jnp.broadcast_to(columns[:, item : item + 1], (width, width))
    for item in range(4):
        sun_ref[item] = jnp.broadcast_to(others[:epochs, item : item + 1], (epochs, width))
    sel_ref[...] = jnp.broadcast_to(others[:blocks, 4:5], (blocks, width))


def put_views(view, first, src, weight, rec):
    width = rec.shape[1]
    scale = src[AREA] * weight * (1.0 / math.pi)
    lanes = pl.ds(first, width)
    for part in range(0, width, 2 * group):
        pieces = []
        for half in range(2):
            at = pl.ds(part + half * group, group)
            dx = rec[0, at, :] - src[PX]
            dy = rec[1, at, :] - src[PY]
            dz = rec[2, at, :] - src[PZ]
            facing = jnp.maximum(
                rec[3, at, :] * dx + rec[4, at, :] * dy + rec[5, at, :] * dz, 0.0
            )
            toward = jnp.maximum(src[NX] * dx + src[NY] * dy + src[NZ] * dz, 0.0)
            spread = dx * dx + dy * dy + dz * dz + src[AREA]
            inverse = 1.0 / spread
            pieces.append(facing * toward * scale * inverse * inverse)
        view[pl.ds(part, 2 * group), lanes] = jnp.concatenate(pieces, 0).astype(jnp.bfloat16)


def origin_of(slot, masks):
    mask = jnp.int32(0)
    for bit in range(len(masks)):
        mask = mask ^ masks[bit] * (slot >> bit & 1)
    return mask


def view_kernel(masks, near_ref, rec, sel, view):
    width = rec.shape[1]
    me = my_block()
    blank = jnp.zeros((group, 1), jnp.float32)

    def block_views(slot, carry):
        src = []
        for item in range(7):
            half, lanes = place_of(item, width)
            src.append(near_ref[slot, pl.ds(half, 1), lanes] + blank)
        weight = row_of(sel, me ^ origin_of(slot, masks), group)
        put_views(view, pl.multiple_of(slot * width, width), src, weight, rec)
        return carry

    lax.fori_loop(0, near_ref.shape[0], block_views, 0, unroll=2)


def step_kernel(
    held,
    per_azimuth,
    masks,
    near_ref,
    far_ref,
    near_view,
    rec,
    sun,
    sel,
    albedo_hbm,
    cond_hbm,
    soil_hbm,
    final_ref,
    bounce_ref,
    tab,
    spot_ref,
    ring,
    flat_ring,
    turned,
    chosen,
    flat_chosen,
    view,
    lit,
    glow,
    find_v,
    find_s,
    load_ref,
    albedo_ref,
    cond_ref,
    soil_ref,
    sems,
):
    pairs = ((albedo_hbm, albedo_ref), (cond_hbm, cond_ref), (soil_hbm, soil_ref))
    late = [
        pltpu.make_async_copy(source, target, sems.at[number])
        for number, (source, target) in enumerate(pairs)
    ]
    for copy in late:
        copy.start()
    blocks = near_ref.shape[0] + far_ref.shape[0]
    width = cond_ref.shape[1]
    epochs = sun.shape[1]
    layers = soil_ref.shape[0]
    f32 = jnp.float32
    me = my_block()

    def unpack(ref, slot, block):
        for item in range(ITEMS):
            half, lanes = place_of(item, width)
            row = ref[slot, pl.ds(half, 1), lanes]
            tab[item, pl.ds(block, 1), :] = row

    def unpack_pair(slot, carry):
        block = me ^ origin_of(slot, masks)
        unpack(near_ref, slot, block)
        unpack(far_ref, slot, block ^ masks[-1])
        return carry

    lax.fori_loop(0, blocks // 2, unpack_pair, 0, unroll=8)

    shift = tab[SAMPLES]
    whole = jnp.maximum(jnp.ceil(shift * (1.0 / width)) - 1.0, 0.0)
    part = shift - whole * width
    double = 2 * blocks
    tabled = turned.shape[0] > group
    if tabled:
        find_v[0] = ((part - 1.0) * (3 * double) + whole).astype(jnp.int32)
    else:
        find_v[0] = whole.astype(jnp.int32)
    find_v[1] = part.astype(jnp.int32)
    lookup = pltpu.make_async_copy(find_v, find_s, sems.at[3])
    lookup.start()

    chunk = min(blocks, 2 * group)
    lane = lax.broadcasted_iota(jnp.int32, (chunk, width), 1)

    def turn_rows(part, near, far):
        rows = jnp.where(lane >= part, near, far)
        return pltpu.roll(rows, (width - part) % width, 1)

    unit = table_unit if tabled else 1.0
    each = -(-width // blocks)
    if tabled:
        east, north = [
            jnp.floor(tab[axis] * unit + 0.5).astype(jnp.int32) for axis in (PX, PY)
        ]
        spot_ref[0] = east.astype(f32)
        spot_ref[1] = north.astype(f32)
        spot_ref[2] = tab[PZ] * unit
        for first in (0, blocks):
            flat_ring[pl.ds(first, blocks), :] = (east << 16) | (north & 0xFFFF)
            ring[pl.ds(first, blocks), :] = spot_ref[2]
        near_flat, far_flat = [flat_ring[pl.ds(first, blocks), :] for first in (0, 1)]
        near_top, far_top = [ring[pl.ds(first, blocks), :] for first in (0, 1)]

        def choose(number, carry):
            keep = lane > number
            flat_chosen[number] = jnp.where(keep, near_flat, far_flat)
            chosen[number] = jnp.where(keep, near_top, far_top)
            return carry

        lax.fori_loop(0, each * blocks, choose, 0, unroll=16)
    else:
        for axis in range(3):
            spot_ref[axis] = tab[axis]
            for first in (0, blocks):
                line = 2 * blocks * axis + first
                ring[pl.ds(line, blocks), :] = tab[axis]

    def turn(block):
        for number in range(each):
            first = block * each + number
            amount = (width - 1 - first) % width
            flat = pltpu.roll(flat_chosen[first], amount, 1)
            top = pltpu.roll(chosen[first], amount, 1)
            east = (flat >> 16).astype(f32)
            north = ((flat << 16) >> 16).astype(f32)
            for axis, rows in enumerate((east, north, top)):
                line = pl.multiple_of((first * 3 + axis) * double, group)
                turned[pl.ds(line, blocks), :] = rows
                turned[pl.ds(line + blocks, blocks), :] = rows
        return jnp.where(east[:group] > 2.0 * table_unit, 1.0, 0.0)

    def view_block(slot, carry):
        block = me ^ origin_of(slot + blocks // 2, masks)
        src = [row_of(tab.at[item], block, group) for item in range(7)]
        weight = row_of(sel, block, group)
        if tabled:
            src[PX] = src[PX] + carry
            carry = turn(2 * slot)
            turn(2 * slot + 1)
        put_views(view, pl.multiple_of(slot * width, width), src, weight, rec)
        return carry

    lax.fori_loop(0, blocks // 2, view_block, jnp.zeros((group, width), f32), unroll=4)

    lookup.wait()

    def azimuth(index, carry):
        line, spot = index // held, (index % held) * per_azimuth
        towards = [row_of(sun.at[item], index, chunk) for item in range(4)]
        for low in range(0, blocks, chunk):
            here = [spot_ref[axis, pl.ds(low, chunk), :] for axis in range(3)]

            def sample(number, best):
                row = find_s[0, line, spot + number] + low
                if tabled:
                    there = [turned[pl.ds(row + axis * double, chunk), :] for axis in range(3)]
                else:
                    part = find_s[1, line, spot + number]
                    there = []
                    for axis in range(3):
                        near = ring[pl.ds(row + axis * double, chunk), :]
                        far = ring[pl.ds(row + 1 + axis * double, chunk), :]
                        there.append(turn_rows(part, near, far))
                dx = there[0] - here[0]
                dy = there[1] - here[1]
                square = jnp.maximum(dx * dx + dy * dy, tiny * unit * unit)
                reach = square * lax.rsqrt(square) + reach_offset * unit
                return jnp.maximum(best, (there[2] - here[2]) / reach)

            start = jnp.full((chunk, width), -1e30, f32)
            horizon = lax.fori_loop(0, per_azimuth, sample, start, unroll=True)
            nx, ny, nz, area, albedo, top = [
                tab[item, pl.ds(low, chunk), :] for item in range(NX, SAMPLES)
            ]
            incidence = towards[0] * nx + towards[1] * ny + towards[2] * nz
            shade = jax.nn.sigmoid((towards[3] - horizon) * (1.0 / shade_width))
            direct = solar_flux * jnp.maximum(incidence, 0.0) * shade
            rows = pl.ds(pl.multiple_of(index * blocks + low, group), chunk)
            lit[rows, :] = direct
            glow[rows, :] = albedo * direct + emissivity * fourth(top)
        return carry

    lax.fori_loop(0, epochs, azimuth, 0, unroll=8)

    def source(pair, flux):
        for views, first in ((near_view, 0), (view, blocks // 2)):
            pieces = []
            for half in range(2):
                block = me ^ origin_of(first + 2 * pair + half, masks)
                piece = glow[pl.ds(block, epochs, stride=blocks), :]
                pieces.append(piece.astype(jnp.bfloat16))
            lanes = pl.ds(pl.multiple_of(pair * (2 * width), 2 * width), 2 * width)
            flux = flux + lax.dot_general(
                jnp.concatenate(pieces, 1),
                views[:, lanes],
                (((1,), (1,)), ((), ())),
                preferred_element_type=f32,
            )
        return flux

    zero = jnp.zeros((epochs, width), f32)
    bounce = lax.fori_loop(0, blocks // 4, source, zero, unroll=4)
    bounce_ref[...] = bounce
    for copy in late:
        copy.wait()
    direct = lit[pl.ds(me, epochs, stride=blocks), :]
    load_ref[...] = (surface_gain * (1.0 - albedo_ref[...])) * (direct + bounce)

    count = layers // group
    slabs = tuple(soil_ref[pl.ds(slab, group, stride=count), :] for slab in range(count))
    sub = lax.broadcasted_iota(jnp.int32, (group, width), 0)
    surface = sub == 0
    inner = sub < group - 1
    loss = jnp.where(surface, surface_gain * emissivity, 0.0)
    cond = cond_ref[...] + jnp.zeros((group, 1), f32)

    def advance(epoch, temps):
        wrapped = pltpu.roll(temps[0], group - 1, 0)
        grads = [temps[i + 1] - temps[i] for i in range(count - 1)]
        grads.append(jnp.where(inner, wrapped - temps[-1], 0.0))
        back = jnp.where(surface, 0.0, pltpu.roll(grads[-1], 1, 0))
        changes = [grads[0] - back] + [grads[i] - grads[i - 1] for i in range(1, count)]
        temps = [temp + cond * change for temp, change in zip(temps, changes)]
        absorbed = jnp.where(surface, row_of(load_ref, epoch, group), 0.0)
        temps[0] = (temps[0] + absorbed) - loss * fourth(temps[0])
        return tuple(temps)

    slabs = lax.fori_loop(0, epochs, advance, slabs, unroll=8)
    for slab in range(count):
        final_ref[pl.ds(slab, group, stride=count), :] = slabs[slab]


def body(positions, normals, area, albedo, conductivity, soil, sun_tan, samples, occupancy):
    width = positions.shape[1]
    axes = ("recv", "src")
    n_recv, n_src = lax.axis_size("recv"), lax.axis_size("src")
    blocks = n_recv * n_src
    epochs = sun_tan.shape[0]
    layers = soil.shape[0]
    held, per_azimuth = samples.shape
    f32 = jnp.float32
    i32 = jnp.int32
    vmem = pl.BlockSpec(memory_space=pltpu.VMEM)
    hbm = pl.BlockSpec(memory_space=pltpu.HBM)
    half = ITEMS // halves * width

    pack = pl.pallas_call(
        pack_kernel,
        out_shape=jax.ShapeDtypeStruct((1, halves, half), f32),
        in_specs=[hbm] * 6,
        out_specs=vmem,
        scratch_shapes=[
            pltpu.VMEM((3, width), f32),
            pltpu.VMEM((3, width), f32),
            pltpu.VMEM((1, width), f32),
            pltpu.VMEM((1, width), f32),
            pltpu.VMEM((group, width), f32),
            pltpu.VMEM((held, per_azimuth), i32),
            pltpu.SemaphoreType.DMA((6,)),
        ],
        compiler_params=pltpu.CompilerParams(vmem_limit_bytes=4 * 2**20),
        name="pack",
    )
    in_hbm = functools.partial(pltpu.with_memory_space_constraint, memory_space=pltpu.HBM)
    near = pack(
        *map(in_hbm, (positions, normals, area[None], albedo[None], soil, samples))
    )

    angle = 2.0 * math.pi * np.arange(epochs) / epochs
    angles = jnp.asarray(np.stack([np.cos(angle), np.sin(angle)]), f32)
    prepare = pl.pallas_call(
        prepare_kernel,
        out_shape=(
            jax.ShapeDtypeStruct((6, width, width), f32),
            jax.ShapeDtypeStruct((4, epochs, width), f32),
            jax.ShapeDtypeStruct((blocks, width), f32),
        ),
        in_specs=[vmem] * 5,
        out_specs=(vmem, vmem, vmem),
        scratch_shapes=[pltpu.VMEM((2, group, width), f32)],
        compiler_params=pltpu.CompilerParams(vmem_limit_bytes=4 * 2**20),
        name="prepare",
    )
    rec, sun, sel = prepare(positions, normals, angles, sun_tan[None], occupancy)

    masks = [n_src << bit | n_src - 1 for bit in reversed(range(n_recv.bit_length() - 1))]
    masks += [1 << bit for bit in reversed(range(n_src.bit_length() - 1))]
    far = None
    for number, mask in enumerate(masks):
        if far is not None:
            near = jnp.concatenate([near, far], 0)
        if number == 2:
            near, rec, sun, sel = lax.optimization_barrier((near, rec, sun, sel))
        far = lax.ppermute(near, axes, [(index, index ^ mask) for index in range(blocks)])

    look = pl.pallas_call(
        functools.partial(view_kernel, masks),
        out_shape=jax.ShapeDtypeStruct((width, blocks // 2 * width), jnp.bfloat16),
        in_specs=[vmem] * 3,
        out_specs=vmem,
        compiler_params=pltpu.CompilerParams(vmem_limit_bytes=2**20),
        name="views",
    )
    near_view = look(near, rec, sel)

    each = -(-width // blocks)
    turned = each * blocks * 3 * 2 * blocks
    tabled = turned * width * 4 <= 2**24
    scratch = [
        ((ITEMS, blocks, width), f32),
        ((3, blocks, width), f32),
        ((2 * blocks * (1 if tabled else 3), width), f32),
        ((2 * blocks, width), i32),
        ((turned if tabled else group, width), f32),
        ((each * blocks, blocks, width) if tabled else (group, width), f32),
        ((each * blocks, blocks, width) if tabled else (group, width), i32),
        ((width, blocks // 2 * width), jnp.bfloat16),
        ((epochs * blocks, width), f32),
        ((epochs * blocks, width), f32),
        ((2, blocks, width), i32),
    ]
    held_bytes = sum(math.prod(shape) * jnp.dtype(kind).itemsize for shape, kind in scratch)
    call = pl.pallas_call(
        functools.partial(step_kernel, held, per_azimuth, masks),
        out_shape=(
            jax.ShapeDtypeStruct((layers, width), f32),
            jax.ShapeDtypeStruct((epochs, width), f32),
        ),
        in_specs=[vmem] * 6 + [hbm] * 3,
        out_specs=(vmem, vmem),
        scratch_shapes=[pltpu.VMEM(*item) for item in scratch]
        + [
            pltpu.SMEM((2, blocks, width), i32),
            pltpu.VMEM((epochs, width), f32),
            pltpu.VMEM((1, width), f32),
            pltpu.VMEM((1, width), f32),
            pltpu.VMEM((layers, width), f32),
            pltpu.SemaphoreType.DMA((4,)),
        ],
        compiler_params=pltpu.CompilerParams(
            vmem_limit_bytes=8 * 2**20 + held_bytes * 5 // 4 + 16 * blocks * half
        ),
        name="step",
    )
    return call(
        near,
        far,
        near_view,
        rec,
        sun,
        sel,
        *map(in_hbm, (albedo[None], conductivity[None], soil)),
    )


def solution(mesh):
    spec = ("basin", "recv", "src")
    in_specs = (
        P(None, spec),
        P(None, spec),
        P(spec),
        P(spec),
        P(spec),
        P(None, spec),
        P(),
        P(spec, None),
        P("basin", None),
    )
    out_specs = (P(None, spec), P(None, spec))
    return jax.shard_map(body, mesh=mesh, in_specs=in_specs, out_specs=out_specs, check_vma=False)
```

```python
import functools
import math

import jax
import jax.numpy as jnp
import numpy as np
from jax import lax
from jax.experimental import pallas as pl
from jax.experimental.pallas import tpu as pltpu
from jax.sharding import PartitionSpec as P

solar_flux = 2.0
emissivity = 0.9
surface_gain = 0.1
shade_width = 0.1
reach_offset = 0.05
tiny = 1e-30
table_unit = 28672.0 * 65536.0

PX, PY, PZ, NX, NY, NZ, AREA, ALBEDO, TOP, SAMPLES, ITEMS = range(11)
halves = 2
group = 8


def fourth(value):
    square = value * value
    return square * square


def row_of(ref, index, count):
    return ref[pl.ds(index, 1), :] + jnp.zeros((count, 1), jnp.float32)


def place_of(item, width):
    per_half = ITEMS // halves
    return item // per_half, pl.ds(item % per_half * width, width)


def pack_kernel(
    pos_hbm,
    nrm_hbm,
    area_hbm,
    albedo_hbm,
    soil_hbm,
    samples_hbm,
    out_ref,
    pos_ref,
    nrm_ref,
    area_ref,
    albedo_ref,
    soil_ref,
    samples_ref,
    sems,
):
    width = pos_ref.shape[1]
    held, count = samples_ref.shape
    pairs = (
        (pos_hbm, pos_ref),
        (nrm_hbm, nrm_ref),
        (area_hbm, area_ref),
        (albedo_hbm, albedo_ref),
        (soil_hbm.at[pl.ds(0, group), :], soil_ref),
        (samples_hbm, samples_ref),
    )
    copies = [
        pltpu.make_async_copy(source, target, sems.at[number])
        for number, (source, target) in enumerate(pairs)
    ]
    for copy in copies:
        copy.start()
    for copy in copies:
        copy.wait()

    def put(item, value):
        half, lanes = place_of(item, width)
        out_ref[0, pl.ds(half, 1), lanes] = value

    for axis in range(3):
        put(PX + axis, pos_ref[pl.ds(axis, 1), :])
        put(NX + axis, nrm_ref[pl.ds(axis, 1), :])
    put(AREA, area_ref[...])
    put(ALBEDO, albedo_ref[...])
    put(TOP, soil_ref[pl.ds(0, 1), :])
    put(SAMPLES, jnp.zeros((1, width), jnp.float32))
    half, lanes = place_of(SAMPLES, width)
    for index in range(held):
        spot = pl.ds(lanes.start + index * count, count)
        out_ref[0, pl.ds(half, 1), spot] = samples_ref[pl.ds(index, 1), :].astype(jnp.float32)


def my_block():
    return lax.axis_index("recv") * lax.axis_size("src") + lax.axis_index("src")


def prepare_kernel(
    pos_ref, nrm_ref, angle_ref, tan_ref, occupancy_ref, rec_ref, sun_ref, sel_ref, stage
):
    width = pos_ref.shape[1]
    epochs = tan_ref.shape[1]
    blocks = occupancy_ref.shape[1]
    me = my_block()
    stage[...] = jnp.zeros_like(stage)
    stage[0, pl.ds(0, 3), :] = pos_ref[...]
    stage[0, pl.ds(3, 3), :] = -nrm_ref[...]
    tangent = tan_ref[...]
    level = lax.rsqrt(1.0 + tangent * tangent)
    stage[1, pl.ds(0, 2), pl.ds(0, epochs)] = angle_ref[...] * level
    stage[1, pl.ds(2, 1), pl.ds(0, epochs)] = tangent * level
    stage[1, pl.ds(3, 1), pl.ds(0, epochs)] = tangent
    stage[1, pl.ds(4, 1), pl.ds(0, blocks)] = occupancy_ref[pl.ds(me, 1), :].astype(jnp.float32)
    columns = stage[0].T
    others = stage[1].T
    for item in range(6):
        rec_ref[item] = jnp.broadcast_to(columns[:, item : item + 1], (width, width))
    for item in range(4):
        sun_ref[item] = jnp.broadcast_to(others[:epochs, item : item + 1], (epochs, width))
    sel_ref[...] = jnp.broadcast_to(others[:blocks, 4:5], (blocks, width))


def put_views(view, first, src, weight, rec, ties=None):
    width = rec.shape[1]
    scale = src[AREA] * weight * (1.0 / math.pi)
    lanes = pl.ds(first, width)
    for part in range(0, width, 2 * group):
        pieces = []
        east = src[PX] if ties is None else src[PX] + ties[part // (2 * group)]
        for half in range(2):
            at = pl.ds(part + half * group, group)
            dx = rec[0, at, :] - east
            dy = rec[1, at, :] - src[PY]
            dz = rec[2, at, :] - src[PZ]
            facing = jnp.maximum(
                rec[3, at, :] * dx + rec[4, at, :] * dy + rec[5, at, :] * dz, 0.0
            )
            toward = jnp.maximum(src[NX] * dx + src[NY] * dy + src[NZ] * dz, 0.0)
            spread = dx * dx + dy * dy + dz * dz + src[AREA]
            inverse = 1.0 / spread
            pieces.append(facing * toward * scale * inverse * inverse)
        view[pl.ds(part, 2 * group), lanes] = jnp.concatenate(pieces, 0).astype(jnp.bfloat16)


def origin_of(slot, masks):
    mask = jnp.int32(0)
    for bit in range(len(masks)):
        mask = mask ^ masks[bit] * (slot >> bit & 1)
    return mask


def view_kernel(masks, near_ref, rec, sel, view):
    width = rec.shape[1]
    me = my_block()
    blank = jnp.zeros((group, 1), jnp.float32)

    def block_views(slot, carry):
        src = []
        for item in range(7):
            half, lanes = place_of(item, width)
            src.append(near_ref[slot, pl.ds(half, 1), lanes] + blank)
        weight = row_of(sel, me ^ origin_of(slot, masks), group)
        put_views(view, pl.multiple_of(slot * width, width), src, weight, rec)
        return carry

    lax.fori_loop(0, near_ref.shape[0], block_views, 0, unroll=2)


def step_kernel(
    held,
    per_azimuth,
    masks,
    near_ref,
    far_ref,
    near_view,
    rec,
    sun,
    sel,
    albedo_hbm,
    cond_hbm,
    soil_hbm,
    final_ref,
    bounce_ref,
    tab,
    spot_ref,
    ring,
    flat_ring,
    turned,
    chosen,
    flat_chosen,
    view,
    lit,
    glow,
    find_v,
    find_s,
    load_ref,
    albedo_ref,
    cond_ref,
    soil_ref,
    sems,
):
    pairs = ((albedo_hbm, albedo_ref), (cond_hbm, cond_ref), (soil_hbm, soil_ref))
    late = [
        pltpu.make_async_copy(source, target, sems.at[number])
        for number, (source, target) in enumerate(pairs)
    ]
    for copy in late:
        copy.start()
    blocks = near_ref.shape[0] + far_ref.shape[0]
    width = cond_ref.shape[1]
    epochs = sun.shape[1]
    layers = soil_ref.shape[0]
    f32 = jnp.float32
    me = my_block()

    def unpack(ref, slot, block):
        for item in range(ITEMS):
            half, lanes = place_of(item, width)
            row = ref[slot, pl.ds(half, 1), lanes]
            tab[item, pl.ds(block, 1), :] = row

    def unpack_pair(slot, carry):
        block = me ^ origin_of(slot, masks)
        unpack(near_ref, slot, block)
        unpack(far_ref, slot, block ^ masks[-1])
        return carry

    lax.fori_loop(0, blocks // 2, unpack_pair, 0, unroll=8)

    shift = tab[SAMPLES]
    whole = jnp.maximum(jnp.ceil(shift * (1.0 / width)) - 1.0, 0.0)
    part = shift - whole * width
    double = 2 * blocks
    tabled = turned.shape[0] > group
    if tabled:
        find_v[0] = ((part - 1.0) * (3 * double) + whole).astype(jnp.int32)
    else:
        find_v[0] = whole.astype(jnp.int32)
    find_v[1] = part.astype(jnp.int32)
    lookup = pltpu.make_async_copy(find_v, find_s, sems.at[3])
    lookup.start()

    chunk = min(blocks, 2 * group)
    lane = lax.broadcasted_iota(jnp.int32, (chunk, width), 1)

    def turn_rows(part, near, far):
        rows = jnp.where(lane >= part, near, far)
        return pltpu.roll(rows, (width - part) % width, 1)

    def unfold(flat):
        return (flat.astype(f32), (flat << 16).astype(f32))

    unit = table_unit if tabled else 1.0
    each = -(-width // blocks)
    if tabled:
        east, north = [
            jnp.floor(tab[axis] * (unit / 65536.0) + 0.5).astype(jnp.int32) for axis in (PX, PY)
        ]
        flat = (east << 16) | (north & 0xFFFF)
        spot_ref[0], spot_ref[1] = unfold(flat)
        spot_ref[0] += 8192.0
        spot_ref[2] = tab[PZ] * unit
        for first in (0, blocks):
            flat_ring[pl.ds(first, blocks), :] = flat
            ring[pl.ds(first, blocks), :] = spot_ref[2]
        near_flat, far_flat = [flat_ring[pl.ds(first, blocks), :] for first in (0, 1)]
        near_top, far_top = [ring[pl.ds(first, blocks), :] for first in (0, 1)]

        def choose(number, carry):
            keep = lane > number
            flat_chosen[number] = jnp.where(keep, near_flat, far_flat)
            chosen[number] = jnp.where(keep, near_top, far_top)
            return carry

        lax.fori_loop(0, each * blocks, choose, 0, unroll=16)
    else:
        for axis in range(3):
            spot_ref[axis] = tab[axis]
            for first in (0, blocks):
                line = 2 * blocks * axis + first
                ring[pl.ds(line, blocks), :] = tab[axis]

    def turn(first):
        amount = (width - 1 - first) % width
        flat = pltpu.roll(flat_chosen[first], amount, 1)
        top = pltpu.roll(chosen[first], amount, 1)
        east, north = unfold(flat)
        for axis, rows in enumerate((east, north, top)):
            line = pl.multiple_of((first * 3 + axis) * double, group)
            turned[pl.ds(line, blocks), :] = rows
            turned[pl.ds(line + blocks, blocks), :] = rows
        return jnp.where(east[:group] > 2.0 * table_unit, 1.0, 0.0)

    parts = width // (2 * group)
    turns = -(-each * blocks // (blocks // 2))

    def view_block(slot, ties):
        block = me ^ origin_of(slot + blocks // 2, masks)
        src = [row_of(tab.at[item], block, group) for item in range(7)]
        weight = row_of(sel, block, group)
        later = list(ties)
        if tabled:
            for number in range(turns):
                later[number * parts // turns] = turn(slot * turns + number)
        first = pl.multiple_of(slot * width, width)
        put_views(view, first, src, weight, rec, ties)
        return tuple(later)

    start = (jnp.zeros((group, width), f32),) * parts
    lax.fori_loop(0, blocks // 2, view_block, start, unroll=2)

    lookup.wait()

    def azimuth(index, carry):
        line, spot = index // held, (index % held) * per_azimuth
        towards = [row_of(sun.at[item], index, chunk) for item in range(4)]
        for low in range(0, blocks, chunk):
            here = [spot_ref[axis, pl.ds(low, chunk), :] for axis in range(3)]

            def sample(number, best):
                row = find_s[0, line, spot + number] + low
                if tabled:
                    there = [turned[pl.ds(row + axis * double, chunk), :] for axis in range(3)]
                else:
                    part = find_s[1, line, spot + number]
                    there = []
                    for axis in range(3):
                        near = ring[pl.ds(row + axis * double, chunk), :]
                        far = ring[pl.ds(row + 1 + axis * double, chunk), :]
                        there.append(turn_rows(part, near, far))
                dx = there[0] - here[0]
                dy = there[1] - here[1]
                square = dx * dx + dy * dy
                if not tabled:
                    square = jnp.maximum(square, tiny)
                reach = square * lax.rsqrt(square) + reach_offset * unit
                return jnp.maximum(best, (there[2] - here[2]) / reach)

            start = jnp.full((chunk, width), -1e30, f32)
            horizon = lax.fori_loop(0, per_azimuth, sample, start, unroll=True)
            nx, ny, nz, area, albedo, top = [
                tab[item, pl.ds(low, chunk), :] for item in range(NX, SAMPLES)
            ]
            incidence = towards[0] * nx + towards[1] * ny + towards[2] * nz
            shade = jax.nn.sigmoid((towards[3] - horizon) * (1.0 / shade_width))
            direct = solar_flux * jnp.maximum(incidence, 0.0) * shade
            rows = pl.ds(pl.multiple_of(index * blocks + low, group), chunk)
            lit[rows, :] = direct
            glow[rows, :] = albedo * direct + emissivity * fourth(top)
        return carry

    lax.fori_loop(0, epochs, azimuth, 0, unroll=8)

    def source(pair, flux):
        for views, first in ((near_view, 0), (view, blocks // 2)):
            pieces = []
            for half in range(2):
                block = me ^ origin_of(first + 2 * pair + half, masks)
                piece = glow[pl.ds(block, epochs, stride=blocks), :]
                pieces.append(piece.astype(jnp.bfloat16))
            lanes = pl.ds(pl.multiple_of(pair * (2 * width), 2 * width), 2 * width)
            flux = flux + lax.dot_general(
                jnp.concatenate(pieces, 1),
                views[:, lanes],
                (((1,), (1,)), ((), ())),
                preferred_element_type=f32,
            )
        return flux

    zero = jnp.zeros((epochs, width), f32)
    bounce = lax.fori_loop(0, blocks // 4, source, zero, unroll=4)
    bounce_ref[...] = bounce
    for copy in late:
        copy.wait()
    direct = lit[pl.ds(me, epochs, stride=blocks), :]
    load_ref[...] = (surface_gain * (1.0 - albedo_ref[...])) * (direct + bounce)

    count = layers // group
    slabs = tuple(soil_ref[pl.ds(slab, group, stride=count), :] for slab in range(count))
    sub = lax.broadcasted_iota(jnp.int32, (group, width), 0)
    surface = sub == 0
    inner = sub < group - 1
    loss = jnp.where(surface, surface_gain * emissivity, 0.0)
    cond = cond_ref[...] + jnp.zeros((group, 1), f32)

    def advance(epoch, temps):
        wrapped = pltpu.roll(temps[0], group - 1, 0)
        grads = [temps[i + 1] - temps[i] for i in range(count - 1)]
        grads.append(jnp.where(inner, wrapped - temps[-1], 0.0))
        back = jnp.where(surface, 0.0, pltpu.roll(grads[-1], 1, 0))
        changes = [grads[0] - back] + [grads[i] - grads[i - 1] for i in range(1, count)]
        temps = [temp + cond * change for temp, change in zip(temps, changes)]
        absorbed = jnp.where(surface, row_of(load_ref, epoch, group), 0.0)
        temps[0] = (temps[0] + absorbed) - loss * fourth(temps[0])
        return tuple(temps)

    slabs = lax.fori_loop(0, epochs, advance, slabs, unroll=8)
    for slab in range(count):
        final_ref[pl.ds(slab, group, stride=count), :] = slabs[slab]


def body(positions, normals, area, albedo, conductivity, soil, sun_tan, samples, occupancy):
    width = positions.shape[1]
    axes = ("recv", "src")
    n_recv, n_src = lax.axis_size("recv"), lax.axis_size("src")
    blocks = n_recv * n_src
    epochs = sun_tan.shape[0]
    layers = soil.shape[0]
    held, per_azimuth = samples.shape
    f32 = jnp.float32
    i32 = jnp.int32
    vmem = pl.BlockSpec(memory_space=pltpu.VMEM)
    hbm = pl.BlockSpec(memory_space=pltpu.HBM)
    half = ITEMS // halves * width

    pack = pl.pallas_call(
        pack_kernel,
        out_shape=jax.ShapeDtypeStruct((1, halves, half), f32),
        in_specs=[hbm] * 6,
        out_specs=vmem,
        scratch_shapes=[
            pltpu.VMEM((3, width), f32),
            pltpu.VMEM((3, width), f32),
            pltpu.VMEM((1, width), f32),
            pltpu.VMEM((1, width), f32),
            pltpu.VMEM((group, width), f32),
            pltpu.VMEM((held, per_azimuth), i32),
            pltpu.SemaphoreType.DMA((6,)),
        ],
        compiler_params=pltpu.CompilerParams(vmem_limit_bytes=4 * 2**20),
        name="pack",
    )
    in_hbm = functools.partial(pltpu.with_memory_space_constraint, memory_space=pltpu.HBM)
    near = pack(
        *map(in_hbm, (positions, normals, area[None], albedo[None], soil, samples))
    )

    angle = 2.0 * math.pi * np.arange(epochs) / epochs
    angles = jnp.asarray(np.stack([np.cos(angle), np.sin(angle)]), f32)
    prepare = pl.pallas_call(
        prepare_kernel,
        out_shape=(
            jax.ShapeDtypeStruct((6, width, width), f32),
            jax.ShapeDtypeStruct((4, epochs, width), f32),
            jax.ShapeDtypeStruct((blocks, width), f32),
        ),
        in_specs=[vmem] * 5,
        out_specs=(vmem, vmem, vmem),
        scratch_shapes=[pltpu.VMEM((2, group, width), f32)],
        compiler_params=pltpu.CompilerParams(vmem_limit_bytes=4 * 2**20),
        name="prepare",
    )
    rec, sun, sel = prepare(positions, normals, angles, sun_tan[None], occupancy)

    masks = [n_src << bit | n_src - 1 for bit in reversed(range(n_recv.bit_length() - 1))]
    masks += [1 << bit for bit in reversed(range(n_src.bit_length() - 1))]
    far = None
    for number, mask in enumerate(masks):
        if far is not None:
            near = jnp.concatenate([near, far], 0)
        if number == 2:
            near, rec, sun, sel = lax.optimization_barrier((near, rec, sun, sel))
        far = lax.ppermute(near, axes, [(index, index ^ mask) for index in range(blocks)])

    look = pl.pallas_call(
        functools.partial(view_kernel, masks),
        out_shape=jax.ShapeDtypeStruct((width, blocks // 2 * width), jnp.bfloat16),
        in_specs=[vmem] * 3,
        out_specs=vmem,
        compiler_params=pltpu.CompilerParams(vmem_limit_bytes=2**20),
        name="views",
    )
    near_view = look(near, rec, sel)

    each = -(-width // blocks)
    turned = each * blocks * 3 * 2 * blocks
    tabled = turned * width * 4 <= 2**24
    scratch = [
        ((ITEMS, blocks, width), f32),
        ((3, blocks, width), f32),
        ((2 * blocks * (1 if tabled else 3), width), f32),
        ((2 * blocks, width), i32),
        ((turned if tabled else group, width), f32),
        ((each * blocks, blocks, width) if tabled else (group, width), f32),
        ((each * blocks, blocks, width) if tabled else (group, width), i32),
        ((width, blocks // 2 * width), jnp.bfloat16),
        ((epochs * blocks, width), f32),
        ((epochs * blocks, width), f32),
        ((2, blocks, width), i32),
    ]
    held_bytes = sum(math.prod(shape) * jnp.dtype(kind).itemsize for shape, kind in scratch)
    call = pl.pallas_call(
        functools.partial(step_kernel, held, per_azimuth, masks),
        out_shape=(
            jax.ShapeDtypeStruct((layers, width), f32),
            jax.ShapeDtypeStruct((epochs, width), f32),
        ),
        in_specs=[vmem] * 6 + [hbm] * 3,
        out_specs=(vmem, vmem),
        scratch_shapes=[pltpu.VMEM(*item) for item in scratch]
        + [
            pltpu.SMEM((2, blocks, width), i32),
            pltpu.VMEM((epochs, width), f32),
            pltpu.VMEM((1, width), f32),
            pltpu.VMEM((1, width), f32),
            pltpu.VMEM((layers, width), f32),
            pltpu.SemaphoreType.DMA((4,)),
        ],
        compiler_params=pltpu.CompilerParams(
            vmem_limit_bytes=8 * 2**20 + held_bytes * 5 // 4 + 16 * blocks * half
        ),
        name="step",
    )
    return call(
        near,
        far,
        near_view,
        rec,
        sun,
        sel,
        *map(in_hbm, (albedo[None], conductivity[None], soil)),
    )


def solution(mesh):
    spec = ("basin", "recv", "src")
    in_specs = (
        P(None, spec),
        P(None, spec),
        P(spec),
        P(spec),
        P(spec),
        P(None, spec),
        P(),
        P(spec, None),
        P("basin", None),
    )
    out_specs = (P(None, spec), P(None, spec))
    return jax.shard_map(body, mesh=mesh, in_specs=in_specs, out_specs=out_specs, check_vma=False)
```

```python
import functools
import math

import jax
import jax.numpy as jnp
import numpy as np
from jax import lax
from jax.experimental import pallas as pl
from jax.experimental.pallas import tpu as pltpu
from jax.sharding import PartitionSpec as P

solar_flux = 2.0
emissivity = 0.9
surface_gain = 0.1
shade_width = 0.1
reach_offset = 0.05
tiny = 1e-30
table_unit = 28672.0 * 65536.0

PX, PY, PZ, NX, NY, NZ, AREA, ALBEDO, TOP, SAMPLES, ITEMS = range(11)
halves = 2
group = 8


def fourth(value):
    square = value * value
    return square * square


def row_of(ref, index, count):
    return ref[pl.ds(index, 1), :] + jnp.zeros((count, 1), jnp.float32)


def place_of(item, width):
    per_half = ITEMS // halves
    return item // per_half, pl.ds(item % per_half * width, width)


def pack_kernel(
    pos_hbm,
    nrm_hbm,
    area_hbm,
    albedo_hbm,
    soil_hbm,
    samples_hbm,
    out_ref,
    pos_ref,
    nrm_ref,
    area_ref,
    albedo_ref,
    soil_ref,
    samples_ref,
    sems,
):
    width = pos_ref.shape[1]
    held, count = samples_ref.shape
    pairs = (
        (pos_hbm, pos_ref),
        (nrm_hbm, nrm_ref),
        (area_hbm, area_ref),
        (albedo_hbm, albedo_ref),
        (soil_hbm.at[pl.ds(0, group), :], soil_ref),
        (samples_hbm, samples_ref),
    )
    copies = [
        pltpu.make_async_copy(source, target, sems.at[number])
        for number, (source, target) in enumerate(pairs)
    ]
    for copy in copies:
        copy.start()
    for copy in copies:
        copy.wait()

    def put(item, value):
        half, lanes = place_of(item, width)
        out_ref[0, pl.ds(half, 1), lanes] = value

    for axis in range(3):
        put(PX + axis, pos_ref[pl.ds(axis, 1), :])
        put(NX + axis, nrm_ref[pl.ds(axis, 1), :])
    put(AREA, area_ref[...])
    put(ALBEDO, albedo_ref[...])
    put(TOP, soil_ref[pl.ds(0, 1), :])
    put(SAMPLES, jnp.zeros((1, width), jnp.float32))
    half, lanes = place_of(SAMPLES, width)
    for index in range(held):
        spot = pl.ds(lanes.start + index * count, count)
        out_ref[0, pl.ds(half, 1), spot] = samples_ref[pl.ds(index, 1), :].astype(jnp.float32)


def my_block():
    return lax.axis_index("recv") * lax.axis_size("src") + lax.axis_index("src")


def prepare_kernel(
    pos_ref, nrm_ref, angle_ref, tan_ref, occupancy_ref, rec_ref, sun_ref, sel_ref, stage
):
    width = pos_ref.shape[1]
    epochs = tan_ref.shape[1]
    blocks = occupancy_ref.shape[1]
    me = my_block()
    stage[...] = jnp.zeros_like(stage)
    stage[0, pl.ds(0, 3), :] = pos_ref[...]
    stage[0, pl.ds(3, 3), :] = -nrm_ref[...]
    tangent = tan_ref[...]
    level = lax.rsqrt(1.0 + tangent * tangent)
    stage[1, pl.ds(0, 2), pl.ds(0, epochs)] = angle_ref[...] * level
    stage[1, pl.ds(2, 1), pl.ds(0, epochs)] = tangent * level
    stage[1, pl.ds(3, 1), pl.ds(0, epochs)] = tangent
    stage[1, pl.ds(4, 1), pl.ds(0, blocks)] = occupancy_ref[pl.ds(me, 1), :].astype(jnp.float32)
    columns = stage[0].T
    others = stage[1].T
    for item in range(6):
        rec_ref[item] = jnp.broadcast_to(columns[:, item : item + 1], (width, width))
    for item in range(4):
        sun_ref[item] = jnp.broadcast_to(others[:epochs, item : item + 1], (epochs, width))
    sel_ref[...] = jnp.broadcast_to(others[:blocks, 4:5], (blocks, width))


def put_views(view, first, src, weight, rec, ties=None):
    width = rec.shape[1]
    scale = src[AREA] * weight * (1.0 / math.pi)
    lanes = pl.ds(first, width)
    for part in range(0, width, 2 * group):
        pieces = []
        east = src[PX] if ties is None else src[PX] + ties[part // (2 * group)]
        for half in range(2):
            at = pl.ds(part + half * group, group)
            dx = rec[0, at, :] - east
            dy = rec[1, at, :] - src[PY]
            dz = rec[2, at, :] - src[PZ]
            facing = jnp.maximum(
                rec[3, at, :] * dx + rec[4, at, :] * dy + rec[5, at, :] * dz, 0.0
            )
            toward = jnp.maximum(src[NX] * dx + src[NY] * dy + src[NZ] * dz, 0.0)
            spread = dx * dx + dy * dy + dz * dz + src[AREA]
            inverse = 1.0 / spread
            pieces.append(facing * toward * scale * inverse * inverse)
        view[pl.ds(part, 2 * group), lanes] = jnp.concatenate(pieces, 0).astype(jnp.bfloat16)


def origin_of(slot, masks):
    mask = jnp.int32(0)
    for bit in range(len(masks)):
        mask = mask ^ masks[bit] * (slot >> bit & 1)
    return mask


def view_kernel(masks, near_ref, rec, sel, view):
    width = rec.shape[1]
    me = my_block()
    blank = jnp.zeros((group, 1), jnp.float32)

    def block_views(slot, carry):
        src = []
        for item in range(7):
            half, lanes = place_of(item, width)
            src.append(near_ref[slot, pl.ds(half, 1), lanes] + blank)
        weight = row_of(sel, me ^ origin_of(slot, masks), group)
        put_views(view, pl.multiple_of(slot * width, width), src, weight, rec)
        return carry

    lax.fori_loop(0, near_ref.shape[0], block_views, 0, unroll=2)


def step_kernel(
    held,
    per_azimuth,
    masks,
    near_ref,
    far_ref,
    near_view,
    rec,
    sun,
    sel,
    albedo_hbm,
    cond_hbm,
    soil_hbm,
    final_ref,
    bounce_ref,
    tab,
    spot_ref,
    ring,
    flat_ring,
    turned,
    view,
    lit,
    glow,
    find_v,
    find_s,
    load_ref,
    albedo_ref,
    cond_ref,
    soil_ref,
    sems,
):
    pairs = ((albedo_hbm, albedo_ref), (cond_hbm, cond_ref), (soil_hbm, soil_ref))
    late = [
        pltpu.make_async_copy(source, target, sems.at[number])
        for number, (source, target) in enumerate(pairs)
    ]
    for copy in late:
        copy.start()
    blocks = near_ref.shape[0] + far_ref.shape[0]
    width = cond_ref.shape[1]
    epochs = sun.shape[1]
    layers = soil_ref.shape[0]
    f32 = jnp.float32
    me = my_block()

    def unpack(ref, slot, block):
        for item in range(ITEMS):
            half, lanes = place_of(item, width)
            row = ref[slot, pl.ds(half, 1), lanes]
            tab[item, pl.ds(block, 1), :] = row

    def unpack_pair(slot, carry):
        block = me ^ origin_of(slot, masks)
        unpack(near_ref, slot, block)
        unpack(far_ref, slot, block ^ masks[-1])
        return carry

    lax.fori_loop(0, blocks // 2, unpack_pair, 0, unroll=8)

    shift = tab[SAMPLES]
    whole = jnp.maximum(jnp.ceil(shift * (1.0 / width)) - 1.0, 0.0)
    part = shift - whole * width
    double = 2 * blocks
    tabled = turned.shape[0] > group
    if tabled:
        find_v[0] = ((part - 1.0) * (3 * double) + whole).astype(jnp.int32)
    else:
        find_v[0] = whole.astype(jnp.int32)
    find_v[1] = part.astype(jnp.int32)
    lookup = pltpu.make_async_copy(find_v, find_s, sems.at[3])
    lookup.start()

    chunk = min(blocks, 2 * group)
    lane = lax.broadcasted_iota(jnp.int32, (chunk, width), 1)

    def turn_rows(part, near, far):
        rows = jnp.where(lane >= part, near, far)
        return pltpu.roll(rows, (width - part) % width, 1)

    def unfold(flat):
        return (flat.astype(f32), (flat << 16).astype(f32))

    unit = table_unit if tabled else 1.0
    each = -(-width // blocks)
    if tabled:
        east, north = [
            jnp.floor(tab[axis] * (unit / 65536.0) + 0.5).astype(jnp.int32) for axis in (PX, PY)
        ]
        flat = (east << 16) | (north & 0xFFFF)
        spot_ref[0], spot_ref[1] = unfold(flat)
        spot_ref[0] += 8192.0
        spot_ref[2] = tab[PZ] * unit
        for first in (0, blocks):
            flat_ring[pl.ds(first, blocks), :] = flat
            ring[pl.ds(first, blocks), :] = spot_ref[2]
    else:
        for axis in range(3):
            spot_ref[axis] = tab[axis]
            for first in (0, blocks):
                line = 2 * blocks * axis + first
                ring[pl.ds(line, blocks), :] = tab[axis]

    def turn(first):
        amount = (width - 1 - first) % width
        keep = lane > first
        flat, top = [
            jnp.where(keep, ref[pl.ds(0, blocks), :], ref[pl.ds(1, blocks), :])
            for ref in (flat_ring, ring)
        ]
        flat = pltpu.roll(flat, amount, 1)
        top = pltpu.roll(top, amount, 1)
        east, north = unfold(flat)
        for axis, rows in enumerate((east, north, top)):
            line = pl.multiple_of((first * 3 + axis) * double, group)
            turned[pl.ds(line, blocks), :] = rows
            turned[pl.ds(line + blocks, blocks), :] = rows
        return jnp.where(east[:group] > 2.0 * table_unit, 1.0, 0.0)

    parts = width // (2 * group)
    turns = -(-each * blocks // (blocks // 2))

    def view_block(slot, ties):
        block = me ^ origin_of(slot + blocks // 2, masks)
        src = [row_of(tab.at[item], block, group) for item in range(7)]
        weight = row_of(sel, block, group)
        later = list(ties)
        if tabled:
            for number in range(turns):
                later[number * parts // turns] = turn(slot * turns + number)
        first = pl.multiple_of(slot * width, width)
        put_views(view, first, src, weight, rec, ties)
        return tuple(later)

    start = (jnp.zeros((group, width), f32),) * parts
    lax.fori_loop(0, blocks // 2, view_block, start, unroll=2)

    lookup.wait()

    def azimuth(index, carry):
        line, spot = index // held, (index % held) * per_azimuth
        towards = [row_of(sun.at[item], index, chunk) for item in range(4)]
        for low in range(0, blocks, chunk):
            here = [spot_ref[axis, pl.ds(low, chunk), :] for axis in range(3)]

            def sample(number, best):
                row = find_s[0, line, spot + number] + low
                if tabled:
                    there = [turned[pl.ds(row + axis * double, chunk), :] for axis in range(3)]
                else:
                    part = find_s[1, line, spot + number]
                    there = []
                    for axis in range(3):
                        near = ring[pl.ds(row + axis * double, chunk), :]
                        far = ring[pl.ds(row + 1 + axis * double, chunk), :]
                        there.append(turn_rows(part, near, far))
                dx = there[0] - here[0]
                dy = there[1] - here[1]
                square = dx * dx + dy * dy
                if not tabled:
                    square = jnp.maximum(square, tiny)
                reach = square * lax.rsqrt(square) + reach_offset * unit
                return jnp.maximum(best, (there[2] - here[2]) / reach)

            start = jnp.full((chunk, width), -1e30, f32)
            horizon = lax.fori_loop(0, per_azimuth, sample, start, unroll=True)
            nx, ny, nz, area, albedo, top = [
                tab[item, pl.ds(low, chunk), :] for item in range(NX, SAMPLES)
            ]
            incidence = towards[0] * nx + towards[1] * ny + towards[2] * nz
            shade = jax.nn.sigmoid((towards[3] - horizon) * (1.0 / shade_width))
            direct = solar_flux * jnp.maximum(incidence, 0.0) * shade
            rows = pl.ds(pl.multiple_of(index * blocks + low, group), chunk)
            lit[rows, :] = direct
            glow[rows, :] = albedo * direct + emissivity * fourth(top)
        return carry

    lax.fori_loop(0, epochs, azimuth, 0, unroll=8)

    def source(pair, flux):
        for views, first in ((near_view, 0), (view, blocks // 2)):
            pieces = []
            for half in range(2):
                block = me ^ origin_of(first + 2 * pair + half, masks)
                piece = glow[pl.ds(block, epochs, stride=blocks), :]
                pieces.append(piece.astype(jnp.bfloat16))
            lanes = pl.ds(pl.multiple_of(pair * (2 * width), 2 * width), 2 * width)
            flux = flux + lax.dot_general(
                jnp.concatenate(pieces, 1),
                views[:, lanes],
                (((1,), (1,)), ((), ())),
                preferred_element_type=f32,
            )
        return flux

    zero = jnp.zeros((epochs, width), f32)
    bounce = lax.fori_loop(0, blocks // 4, source, zero, unroll=4)
    bounce_ref[...] = bounce
    for copy in late:
        copy.wait()
    direct = lit[pl.ds(me, epochs, stride=blocks), :]
    load_ref[...] = (surface_gain * (1.0 - albedo_ref[...])) * (direct + bounce)

    count = layers // group
    slabs = tuple(soil_ref[pl.ds(slab, group, stride=count), :] for slab in range(count))
    sub = lax.broadcasted_iota(jnp.int32, (group, width), 0)
    surface = sub == 0
    inner = sub < group - 1
    loss = jnp.where(surface, surface_gain * emissivity, 0.0)
    cond = cond_ref[...] + jnp.zeros((group, 1), f32)

    def advance(epoch, temps):
        wrapped = pltpu.roll(temps[0], group - 1, 0)
        grads = [temps[i + 1] - temps[i] for i in range(count - 1)]
        grads.append(jnp.where(inner, wrapped - temps[-1], 0.0))
        back = jnp.where(surface, 0.0, pltpu.roll(grads[-1], 1, 0))
        changes = [grads[0] - back] + [grads[i] - grads[i - 1] for i in range(1, count)]
        temps = [temp + cond * change for temp, change in zip(temps, changes)]
        absorbed = jnp.where(surface, row_of(load_ref, epoch, group), 0.0)
        temps[0] = (temps[0] + absorbed) - loss * fourth(temps[0])
        return tuple(temps)

    slabs = lax.fori_loop(0, epochs, advance, slabs, unroll=8)
    for slab in range(count):
        final_ref[pl.ds(slab, group, stride=count), :] = slabs[slab]


def body(positions, normals, area, albedo, conductivity, soil, sun_tan, samples, occupancy):
    width = positions.shape[1]
    axes = ("recv", "src")
    n_recv, n_src = lax.axis_size("recv"), lax.axis_size("src")
    blocks = n_recv * n_src
    epochs = sun_tan.shape[0]
    layers = soil.shape[0]
    held, per_azimuth = samples.shape
    f32 = jnp.float32
    i32 = jnp.int32
    vmem = pl.BlockSpec(memory_space=pltpu.VMEM)
    hbm = pl.BlockSpec(memory_space=pltpu.HBM)
    half = ITEMS // halves * width

    pack = pl.pallas_call(
        pack_kernel,
        out_shape=jax.ShapeDtypeStruct((1, halves, half), f32),
        in_specs=[hbm] * 6,
        out_specs=vmem,
        scratch_shapes=[
            pltpu.VMEM((3, width), f32),
            pltpu.VMEM((3, width), f32),
            pltpu.VMEM((1, width), f32),
            pltpu.VMEM((1, width), f32),
            pltpu.VMEM((group, width), f32),
            pltpu.VMEM((held, per_azimuth), i32),
            pltpu.SemaphoreType.DMA((6,)),
        ],
        compiler_params=pltpu.CompilerParams(vmem_limit_bytes=4 * 2**20),
        name="pack",
    )
    in_hbm = functools.partial(pltpu.with_memory_space_constraint, memory_space=pltpu.HBM)
    near = pack(
        *map(in_hbm, (positions, normals, area[None], albedo[None], soil, samples))
    )

    angle = 2.0 * math.pi * np.arange(epochs) / epochs
    angles = jnp.asarray(np.stack([np.cos(angle), np.sin(angle)]), f32)
    prepare = pl.pallas_call(
        prepare_kernel,
        out_shape=(
            jax.ShapeDtypeStruct((6, width, width), f32),
            jax.ShapeDtypeStruct((4, epochs, width), f32),
            jax.ShapeDtypeStruct((blocks, width), f32),
        ),
        in_specs=[vmem] * 5,
        out_specs=(vmem, vmem, vmem),
        scratch_shapes=[pltpu.VMEM((2, group, width), f32)],
        compiler_params=pltpu.CompilerParams(vmem_limit_bytes=4 * 2**20),
        name="prepare",
    )
    rec, sun, sel = prepare(positions, normals, angles, sun_tan[None], occupancy)

    masks = [n_src << bit | n_src - 1 for bit in reversed(range(n_recv.bit_length() - 1))]
    masks += [1 << bit for bit in reversed(range(n_src.bit_length() - 1))]
    far = None
    for number, mask in enumerate(masks):
        if far is not None:
            near = jnp.concatenate([near, far], 0)
        if number == 2:
            near, rec, sun, sel = lax.optimization_barrier((near, rec, sun, sel))
        far = lax.ppermute(near, axes, [(index, index ^ mask) for index in range(blocks)])

    look = pl.pallas_call(
        functools.partial(view_kernel, masks),
        out_shape=jax.ShapeDtypeStruct((width, blocks // 2 * width), jnp.bfloat16),
        in_specs=[vmem] * 3,
        out_specs=vmem,
        compiler_params=pltpu.CompilerParams(vmem_limit_bytes=2**20),
        name="views",
    )
    near_view = look(near, rec, sel)

    each = -(-width // blocks)
    turned = each * blocks * 3 * 2 * blocks
    tabled = turned * width * 4 <= 2**24
    scratch = [
        ((ITEMS, blocks, width), f32),
        ((3, blocks, width), f32),
        ((2 * blocks * (1 if tabled else 3), width), f32),
        ((2 * blocks, width), i32),
        ((turned if tabled else group, width), f32),
        ((width, blocks // 2 * width), jnp.bfloat16),
        ((epochs * blocks, width), f32),
        ((epochs * blocks, width), f32),
        ((2, blocks, width), i32),
    ]
    held_bytes = sum(math.prod(shape) * jnp.dtype(kind).itemsize for shape, kind in scratch)
    call = pl.pallas_call(
        functools.partial(step_kernel, held, per_azimuth, masks),
        out_shape=(
            jax.ShapeDtypeStruct((layers, width), f32),
            jax.ShapeDtypeStruct((epochs, width), f32),
        ),
        in_specs=[vmem] * 6 + [hbm] * 3,
        out_specs=(vmem, vmem),
        scratch_shapes=[pltpu.VMEM(*item) for item in scratch]
        + [
            pltpu.SMEM((2, blocks, width), i32),
            pltpu.VMEM((epochs, width), f32),
            pltpu.VMEM((1, width), f32),
            pltpu.VMEM((1, width), f32),
            pltpu.VMEM((layers, width), f32),
            pltpu.SemaphoreType.DMA((4,)),
        ],
        compiler_params=pltpu.CompilerParams(
            vmem_limit_bytes=8 * 2**20 + held_bytes * 5 // 4 + 16 * blocks * half
        ),
        name="step",
    )
    return call(
        near,
        far,
        near_view,
        rec,
        sun,
        sel,
        *map(in_hbm, (albedo[None], conductivity[None], soil)),
    )


def solution(mesh):
    spec = ("basin", "recv", "src")
    in_specs = (
        P(None, spec),
        P(None, spec),
        P(spec),
        P(spec),
        P(spec),
        P(None, spec),
        P(),
        P(spec, None),
        P("basin", None),
    )
    out_specs = (P(None, spec), P(None, spec))
    return jax.shard_map(body, mesh=mesh, in_specs=in_specs, out_specs=out_specs, check_vma=False)
```

```python
import functools
import math

import jax
import jax.numpy as jnp
import numpy as np
from jax import lax
from jax.experimental import pallas as pl
from jax.experimental.pallas import tpu as pltpu
from jax.sharding import PartitionSpec as P

solar_flux = 2.0
emissivity = 0.9
surface_gain = 0.1
shade_width = 0.1
reach_offset = 0.05
tiny = 1e-30
table_unit = 28672.0 * 65536.0

PX, PY, PZ, NX, NY, NZ, AREA, ALBEDO, TOP, SAMPLES, ITEMS = range(11)
halves = 2
group = 8


def fourth(value):
    square = value * value
    return square * square


def row_of(ref, index, count):
    return ref[pl.ds(index, 1), :] + jnp.zeros((count, 1), jnp.float32)


def place_of(item, width):
    per_half = ITEMS // halves
    return item // per_half, pl.ds(item % per_half * width, width)


def pack_kernel(
    pos_hbm,
    nrm_hbm,
    area_hbm,
    albedo_hbm,
    soil_hbm,
    samples_hbm,
    out_ref,
    pos_ref,
    nrm_ref,
    area_ref,
    albedo_ref,
    soil_ref,
    samples_ref,
    sems,
):
    width = pos_ref.shape[1]
    held, count = samples_ref.shape
    pairs = (
        (pos_hbm, pos_ref),
        (nrm_hbm, nrm_ref),
        (area_hbm, area_ref),
        (albedo_hbm, albedo_ref),
        (soil_hbm.at[pl.ds(0, group), :], soil_ref),
        (samples_hbm, samples_ref),
    )
    copies = [
        pltpu.make_async_copy(source, target, sems.at[number])
        for number, (source, target) in enumerate(pairs)
    ]
    for copy in copies:
        copy.start()
    for copy in copies:
        copy.wait()

    def put(item, value):
        half, lanes = place_of(item, width)
        out_ref[0, pl.ds(half, 1), lanes] = value

    for axis in range(3):
        put(PX + axis, pos_ref[pl.ds(axis, 1), :])
        put(NX + axis, nrm_ref[pl.ds(axis, 1), :])
    put(AREA, area_ref[...])
    put(ALBEDO, albedo_ref[...])
    put(TOP, soil_ref[pl.ds(0, 1), :])
    put(SAMPLES, jnp.zeros((1, width), jnp.float32))
    half, lanes = place_of(SAMPLES, width)
    for index in range(held):
        spot = pl.ds(lanes.start + index * count, count)
        out_ref[0, pl.ds(half, 1), spot] = samples_ref[pl.ds(index, 1), :].astype(jnp.float32)


def my_block():
    return lax.axis_index("recv") * lax.axis_size("src") + lax.axis_index("src")


def prepare_kernel(
    pos_ref, nrm_ref, angle_ref, tan_ref, occupancy_ref, rec_ref, sun_ref, sel_ref, stage
):
    width = pos_ref.shape[1]
    epochs = tan_ref.shape[1]
    blocks = occupancy_ref.shape[1]
    me = my_block()
    stage[...] = jnp.zeros_like(stage)
    stage[0, pl.ds(0, 3), :] = pos_ref[...]
    stage[0, pl.ds(3, 3), :] = -nrm_ref[...]
    tangent = tan_ref[...]
    level = solar_flux * lax.rsqrt(1.0 + tangent * tangent)
    stage[1, pl.ds(0, 2), pl.ds(0, epochs)] = angle_ref[...] * level
    stage[1, pl.ds(2, 1), pl.ds(0, epochs)] = tangent * level
    stage[1, pl.ds(3, 1), pl.ds(0, epochs)] = tangent
    stage[1, pl.ds(4, 1), pl.ds(0, blocks)] = occupancy_ref[pl.ds(me, 1), :].astype(jnp.float32)
    columns = stage[0].T
    others = stage[1].T
    for item in range(6):
        rec_ref[item] = jnp.broadcast_to(columns[:, item : item + 1], (width, width))
    for item in range(4):
        sun_ref[item] = jnp.broadcast_to(others[:epochs, item : item + 1], (epochs, width))
    sel_ref[...] = jnp.broadcast_to(others[:blocks, 4:5], (blocks, width))


def put_views(view, first, src, weight, rec, ties=None):
    width = rec.shape[1]
    scale = src[AREA] * weight * (1.0 / math.pi)
    lanes = pl.ds(first, width)
    for part in range(0, width, 2 * group):
        pieces = []
        east = src[PX] if ties is None else src[PX] + ties[part // (2 * group)]
        for half in range(2):
            at = pl.ds(part + half * group, group)
            dx = rec[0, at, :] - east
            dy = rec[1, at, :] - src[PY]
            dz = rec[2, at, :] - src[PZ]
            facing = jnp.maximum(
                rec[3, at, :] * dx + rec[4, at, :] * dy + rec[5, at, :] * dz, 0.0
            )
            toward = jnp.maximum(src[NX] * dx + src[NY] * dy + src[NZ] * dz, 0.0)
            spread = dx * dx + dy * dy + dz * dz + src[AREA]
            inverse = 1.0 / spread
            pieces.append(facing * toward * scale * inverse * inverse)
        view[pl.ds(part, 2 * group), lanes] = jnp.concatenate(pieces, 0).astype(jnp.bfloat16)


def origin_of(slot, masks):
    mask = jnp.int32(0)
    for bit in range(len(masks)):
        mask = mask ^ masks[bit] * (slot >> bit & 1)
    return mask


def view_kernel(masks, near_ref, rec, sel, view):
    width = rec.shape[1]
    me = my_block()
    blank = jnp.zeros((group, 1), jnp.float32)

    def block_views(slot, carry):
        src = []
        for item in range(7):
            half, lanes = place_of(item, width)
            src.append(near_ref[slot, pl.ds(half, 1), lanes] + blank)
        weight = row_of(sel, me ^ origin_of(slot, masks), group)
        put_views(view, pl.multiple_of(slot * width, width), src, weight, rec)
        return carry

    lax.fori_loop(0, near_ref.shape[0], block_views, 0, unroll=2)


def step_kernel(
    held,
    per_azimuth,
    masks,
    near_ref,
    far_ref,
    near_view,
    rec,
    sun,
    sel,
    albedo_hbm,
    cond_hbm,
    soil_hbm,
    final_ref,
    bounce_ref,
    tab,
    spot_ref,
    ring,
    flat_ring,
    turned,
    view,
    lit,
    glow,
    find_v,
    find_s,
    load_ref,
    albedo_ref,
    cond_ref,
    soil_ref,
    sems,
):
    pairs = ((albedo_hbm, albedo_ref), (cond_hbm, cond_ref), (soil_hbm, soil_ref))
    late = [
        pltpu.make_async_copy(source, target, sems.at[number])
        for number, (source, target) in enumerate(pairs)
    ]
    for copy in late:
        copy.start()
    blocks = near_ref.shape[0] + far_ref.shape[0]
    width = cond_ref.shape[1]
    epochs = sun.shape[1]
    layers = soil_ref.shape[0]
    f32 = jnp.float32
    me = my_block()

    def unpack(ref, slot, block):
        for item in range(ITEMS):
            half, lanes = place_of(item, width)
            row = ref[slot, pl.ds(half, 1), lanes]
            tab[item, pl.ds(block, 1), :] = row

    def unpack_pair(slot, carry):
        block = me ^ origin_of(slot, masks)
        unpack(near_ref, slot, block)
        unpack(far_ref, slot, block ^ masks[-1])
        return carry

    lax.fori_loop(0, blocks // 2, unpack_pair, 0, unroll=8)

    shift = tab[SAMPLES]
    whole = jnp.maximum(jnp.ceil(shift * (1.0 / width)) - 1.0, 0.0)
    part = shift - whole * width
    double = 2 * blocks
    tabled = turned.shape[0] > group
    if tabled:
        find_v[0] = ((part - 1.0) * (3 * double) + whole).astype(jnp.int32)
    else:
        find_v[0] = whole.astype(jnp.int32)
    find_v[1] = part.astype(jnp.int32)
    lookup = pltpu.make_async_copy(find_v, find_s, sems.at[3])
    lookup.start()

    chunk = min(blocks, 2 * group)
    lane = lax.broadcasted_iota(jnp.int32, (chunk, width), 1)

    def turn_rows(part, near, far):
        rows = jnp.where(lane >= part, near, far)
        return pltpu.roll(rows, (width - part) % width, 1)

    def unfold(flat):
        return (flat.astype(f32), (flat << 16).astype(f32))

    unit = table_unit if tabled else 1.0
    each = -(-width // blocks)
    if tabled:
        east, north = [
            jnp.floor(tab[axis] * (unit / 65536.0) + 0.5).astype(jnp.int32) for axis in (PX, PY)
        ]
        flat = (east << 16) | (north & 0xFFFF)
        spot_ref[0], spot_ref[1] = unfold(flat)
        spot_ref[0] += 8192.0
        spot_ref[2] = tab[PZ] * unit
        for first in (0, blocks):
            flat_ring[pl.ds(first, blocks), :] = flat
            ring[pl.ds(first, blocks), :] = spot_ref[2]
    else:
        for axis in range(3):
            spot_ref[axis] = tab[axis]
            for first in (0, blocks):
                line = 2 * blocks * axis + first
                ring[pl.ds(line, blocks), :] = tab[axis]

    def turn(first):
        amount = (width - 1 - first) % width
        keep = lane > first
        flat, top = [
            jnp.where(keep, ref[pl.ds(0, blocks), :], ref[pl.ds(1, blocks), :])
            for ref in (flat_ring, ring)
        ]
        flat = pltpu.roll(flat, amount, 1)
        top = pltpu.roll(top, amount, 1)
        east, north = unfold(flat)
        for axis, rows in enumerate((east, north, top)):
            line = pl.multiple_of((first * 3 + axis) * double, group)
            turned[pl.ds(line, blocks), :] = rows
            turned[pl.ds(line + blocks, blocks), :] = rows
        return jnp.where(east[:group] > 2.0 * table_unit, 1.0, 0.0)

    parts = width // (2 * group)
    turns = -(-each * blocks // (blocks // 2))

    def view_block(slot, ties):
        block = me ^ origin_of(slot + blocks // 2, masks)
        src = [row_of(tab.at[item], block, group) for item in range(7)]
        weight = row_of(sel, block, group)
        later = list(ties)
        if tabled:
            for number in range(turns):
                later[number * parts // turns] = turn(slot * turns + number)
        first = pl.multiple_of(slot * width, width)
        put_views(view, first, src, weight, rec, ties)
        return tuple(later)

    start = (jnp.zeros((group, width), f32),) * parts
    lax.fori_loop(0, blocks // 2, view_block, start, unroll=2)

    lookup.wait()
    tab[TOP] = emissivity * fourth(tab[TOP])

    def azimuth(index, carry):
        line, spot = index // held, (index % held) * per_azimuth
        towards = [row_of(sun.at[item], index, chunk) for item in range(4)]
        for low in range(0, blocks, chunk):
            here = [spot_ref[axis, pl.ds(low, chunk), :] for axis in range(3)]

            def sample(number, best):
                row = find_s[0, line, spot + number] + low
                if tabled:
                    there = [turned[pl.ds(row + axis * double, chunk), :] for axis in range(3)]
                else:
                    part = find_s[1, line, spot + number]
                    there = []
                    for axis in range(3):
                        near = ring[pl.ds(row + axis * double, chunk), :]
                        far = ring[pl.ds(row + 1 + axis * double, chunk), :]
                        there.append(turn_rows(part, near, far))
                dx = there[0] - here[0]
                dy = there[1] - here[1]
                square = dx * dx + dy * dy
                if not tabled:
                    square = jnp.maximum(square, tiny)
                reach = square * lax.rsqrt(square) + reach_offset * unit
                return jnp.maximum(best, (there[2] - here[2]) / reach)

            start = jnp.full((chunk, width), -1e30, f32)
            horizon = lax.fori_loop(0, per_azimuth, sample, start, unroll=True)
            nx, ny, nz, area, albedo, top = [
                tab[item, pl.ds(low, chunk), :] for item in range(NX, SAMPLES)
            ]
            incidence = towards[0] * nx + towards[1] * ny + towards[2] * nz
            shade = jax.nn.sigmoid((towards[3] - horizon) * (1.0 / shade_width))
            direct = jnp.maximum(incidence, 0.0) * shade
            rows = pl.ds(low * epochs + index, chunk, stride=epochs)
            lit[rows, :] = direct
            glow[rows, :] = albedo * direct + top
        return carry

    lax.fori_loop(0, epochs, azimuth, 0, unroll=8)

    def source(pair, flux):
        for views, first in ((near_view, 0), (view, blocks // 2)):
            pieces = []
            for half in range(2):
                block = me ^ origin_of(first + 2 * pair + half, masks)
                piece = glow[pl.ds(pl.multiple_of(block * epochs, group), epochs), :]
                pieces.append(piece.astype(jnp.bfloat16))
            lanes = pl.ds(pl.multiple_of(pair * (2 * width), 2 * width), 2 * width)
            flux = flux + lax.dot_general(
                jnp.concatenate(pieces, 1),
                views[:, lanes],
                (((1,), (1,)), ((), ())),
                preferred_element_type=f32,
            )
        return flux

    zero = jnp.zeros((epochs, width), f32)
    bounce = lax.fori_loop(0, blocks // 4, source, zero, unroll=4)
    bounce_ref[...] = bounce
    for copy in late:
        copy.wait()
    direct = lit[pl.ds(pl.multiple_of(me * epochs, group), epochs), :]
    load_ref[...] = (surface_gain * (1.0 - albedo_ref[...])) * (direct + bounce)

    count = layers // group
    slabs = tuple(soil_ref[pl.ds(slab, group, stride=count), :] for slab in range(count))
    sub = lax.broadcasted_iota(jnp.int32, (group, width), 0)
    surface = sub == 0
    inner = sub < group - 1
    loss = jnp.where(surface, surface_gain * emissivity, 0.0)
    cond = cond_ref[...] + jnp.zeros((group, 1), f32)

    def advance(epoch, temps):
        wrapped = pltpu.roll(temps[0], group - 1, 0)
        grads = [temps[i + 1] - temps[i] for i in range(count - 1)]
        grads.append(jnp.where(inner, wrapped - temps[-1], 0.0))
        back = jnp.where(surface, 0.0, pltpu.roll(grads[-1], 1, 0))
        changes = [grads[0] - back] + [grads[i] - grads[i - 1] for i in range(1, count)]
        temps = [temp + cond * change for temp, change in zip(temps, changes)]
        absorbed = jnp.where(surface, row_of(load_ref, epoch, group), 0.0)
        temps[0] = (temps[0] + absorbed) - loss * fourth(temps[0])
        return tuple(temps)

    slabs = lax.fori_loop(0, epochs, advance, slabs, unroll=8)
    for slab in range(count):
        final_ref[pl.ds(slab, group, stride=count), :] = slabs[slab]


def body(positions, normals, area, albedo, conductivity, soil, sun_tan, samples, occupancy):
    width = positions.shape[1]
    axes = ("recv", "src")
    n_recv, n_src = lax.axis_size("recv"), lax.axis_size("src")
    blocks = n_recv * n_src
    epochs = sun_tan.shape[0]
    layers = soil.shape[0]
    held, per_azimuth = samples.shape
    f32 = jnp.float32
    i32 = jnp.int32
    vmem = pl.BlockSpec(memory_space=pltpu.VMEM)
    hbm = pl.BlockSpec(memory_space=pltpu.HBM)
    half = ITEMS // halves * width

    pack = pl.pallas_call(
        pack_kernel,
        out_shape=jax.ShapeDtypeStruct((1, halves, half), f32),
        in_specs=[hbm] * 6,
        out_specs=vmem,
        scratch_shapes=[
            pltpu.VMEM((3, width), f32),
            pltpu.VMEM((3, width), f32),
            pltpu.VMEM((1, width), f32),
            pltpu.VMEM((1, width), f32),
            pltpu.VMEM((group, width), f32),
            pltpu.VMEM((held, per_azimuth), i32),
            pltpu.SemaphoreType.DMA((6,)),
        ],
        compiler_params=pltpu.CompilerParams(vmem_limit_bytes=4 * 2**20),
        name="pack",
    )
    in_hbm = functools.partial(pltpu.with_memory_space_constraint, memory_space=pltpu.HBM)
    near = pack(
        *map(in_hbm, (positions, normals, area[None], albedo[None], soil, samples))
    )

    angle = 2.0 * math.pi * np.arange(epochs) / epochs
    angles = jnp.asarray(np.stack([np.cos(angle), np.sin(angle)]), f32)
    prepare = pl.pallas_call(
        prepare_kernel,
        out_shape=(
            jax.ShapeDtypeStruct((6, width, width), f32),
            jax.ShapeDtypeStruct((4, epochs, width), f32),
            jax.ShapeDtypeStruct((blocks, width), f32),
        ),
        in_specs=[vmem] * 5,
        out_specs=(vmem, vmem, vmem),
        scratch_shapes=[pltpu.VMEM((2, group, width), f32)],
        compiler_params=pltpu.CompilerParams(vmem_limit_bytes=4 * 2**20),
        name="prepare",
    )
    rec, sun, sel = prepare(positions, normals, angles, sun_tan[None], occupancy)

    masks = [n_src << bit | n_src - 1 for bit in reversed(range(n_recv.bit_length() - 1))]
    masks += [1 << bit for bit in reversed(range(n_src.bit_length() - 1))]
    far = None
    for number, mask in enumerate(masks):
        if far is not None:
            near = jnp.concatenate([near, far], 0)
        if number == 2:
            near, rec, sun, sel = lax.optimization_barrier((near, rec, sun, sel))
        far = lax.ppermute(near, axes, [(index, index ^ mask) for index in range(blocks)])

    look = pl.pallas_call(
        functools.partial(view_kernel, masks),
        out_shape=jax.ShapeDtypeStruct((width, blocks // 2 * width), jnp.bfloat16),
        in_specs=[vmem] * 3,
        out_specs=vmem,
        compiler_params=pltpu.CompilerParams(vmem_limit_bytes=2**20),
        name="views",
    )
    near_view = look(near, rec, sel)

    each = -(-width // blocks)
    turned = each * blocks * 3 * 2 * blocks
    tabled = turned * width * 4 <= 2**24
    scratch = [
        ((ITEMS, blocks, width), f32),
        ((3, blocks, width), f32),
        ((2 * blocks * (1 if tabled else 3), width), f32),
        ((2 * blocks, width), i32),
        ((turned if tabled else group, width), f32),
        ((width, blocks // 2 * width), jnp.bfloat16),
        ((epochs * blocks, width), f32),
        ((epochs * blocks, width), f32),
        ((2, blocks, width), i32),
    ]
    held_bytes = sum(math.prod(shape) * jnp.dtype(kind).itemsize for shape, kind in scratch)
    call = pl.pallas_call(
        functools.partial(step_kernel, held, per_azimuth, masks),
        out_shape=(
            jax.ShapeDtypeStruct((layers, width), f32),
            jax.ShapeDtypeStruct((epochs, width), f32),
        ),
        in_specs=[vmem] * 6 + [hbm] * 3,
        out_specs=(vmem, vmem),
        scratch_shapes=[pltpu.VMEM(*item) for item in scratch]
        + [
            pltpu.SMEM((2, blocks, width), i32),
            pltpu.VMEM((epochs, width), f32),
            pltpu.VMEM((1, width), f32),
            pltpu.VMEM((1, width), f32),
            pltpu.VMEM((layers, width), f32),
            pltpu.SemaphoreType.DMA((4,)),
        ],
        compiler_params=pltpu.CompilerParams(
            vmem_limit_bytes=8 * 2**20 + held_bytes * 5 // 4 + 16 * blocks * half
        ),
        name="step",
    )
    return call(
        near,
        far,
        near_view,
        rec,
        sun,
        sel,
        *map(in_hbm, (albedo[None], conductivity[None], soil)),
    )


def solution(mesh):
    spec = ("basin", "recv", "src")
    in_specs = (
        P(None, spec),
        P(None, spec),
        P(spec),
        P(spec),
        P(spec),
        P(None, spec),
        P(),
        P(spec, None),
        P("basin", None),
    )
    out_specs = (P(None, spec), P(None, spec))
    return jax.shard_map(body, mesh=mesh, in_specs=in_specs, out_specs=out_specs, check_vma=False)
```
